128 devices in a mesh: lat: 8 (over z, x_lo), lon: 16 (over y, x_hi, core).
Axes of the slice: x: 4 (x_hi: 2, x_lo: 2; x = x_hi * 2 + x_lo), y: 4, z: 4, core: 2. Of those that a mesh axis runs over, the one named last changes fastest.
Arguments:
- features: bfloat16 [128, 512, 768], P('lat', 'lon'), may hold values from -10 to 10
- grad_output: bfloat16 [128, 512, 768], P('lat', 'lon'), may hold values from -6 to 6
- qkv_weight: bfloat16 [768, 2304], P(('lat', 'lon')), may hold values from -0.5 to 0.5
- out_weight: bfloat16 [768, 768], P(('lat', 'lon')), may hold values from -0.21875 to 0.21875
Outputs:
- grad_features: bfloat16 [128, 512, 768], P('lat', 'lon')
- grad_qkv_weight: float32 [768, 2304], P(('lat', 'lon'))
- grad_out_weight: float32 [768, 768], P(('lat', 'lon'))
The draws below stay inside these ranges and needn't reach their ends.
All inputs are finite; a program needn't handle non-finite values.
Results may differ from the reference program's by a relative error of at most 0.018.
Values may be sent and summed in bfloat16 or wider, within the bound.
A program may use at most 128 MiB of HBM per device.

```python
import math
import jax
import jax.numpy as jnp
from jax import lax

D = 768
HEADS = 12
RADIUS = 6
QROWS = 16
QCOLS = 16
NLAT = 128
NLON = 512


def draw_features(key, part):
    values_f32 = jnp.clip(jax.random.normal(key, (NLAT, NLON, D), jnp.float32), -6.0, 6.0)
    return values_f32.astype(jnp.bfloat16)


def draw_qkv_weight(key, part):
    values_f32 = jax.random.normal(key, (D, 3 * D), jnp.float32) * (1.0 / math.sqrt(D))
    return jnp.clip(values_f32, -0.5, 0.5).astype(jnp.bfloat16)


def levels(key, shape, pieces, least, top_value):
    def one(axis_at, blocks):
        heights = jax.random.uniform(jax.random.fold_in(jax.random.fold_in(key, 6), axis_at), (blocks,), jnp.float32, least / len(pieces), top_value / len(pieces))
        return jnp.repeat(jnp.exp(heights), shape[axis_at] // blocks).reshape((-1,) + (1,) * (len(shape) - axis_at - 1))

    loudness = one(*pieces[0])
    for cut in pieces[1:]:
        loudness = loudness * one(*cut)
    return loudness


def gaussian(own_key, dims, spread, most, shards=(), kind=jnp.bfloat16):
    array = spread * jax.random.normal(own_key, dims, jnp.float32)
    if shards:
        array = array * levels(own_key, dims, shards, -0.22, 0.18)
    return jnp.clip(array, -most, most).astype(kind)


def setup_inputs(seed: int = 0) -> dict:
    arg_keys = jax.random.split(jax.random.key(seed), 5)
    return {
        "features": draw_features(jax.random.fold_in(arg_keys[4], 71), 0),
        "grad_output": gaussian(arg_keys[1], (NLAT, NLON, D), 1.0, 6.0, ((0, 8), (1, 16))),
        "qkv_weight": draw_qkv_weight(jax.random.fold_in(arg_keys[4], 71), 0),
        "out_weight": gaussian(arg_keys[3], (D, D), D ** -0.5, 0.21875, ((0, 128),)),
    }


def window_mask(row_first, query_rows, query_cols, key_rows, key_cols, radius, total_rows):
    q_rows = row_first + jnp.arange(query_rows, dtype=jnp.int32)
    k_rows = row_first - radius + jnp.arange(key_rows, dtype=jnp.int32)
    row_start = jnp.clip(q_rows - radius, 0, total_rows - 2 * radius - 1)
    row_valid = (k_rows[None, :] >= row_start[:, None]) & (k_rows[None, :] <= row_start[:, None] + 2 * radius)
    q_cols = jnp.arange(query_cols, dtype=jnp.int32)
    k_cols = jnp.arange(key_cols, dtype=jnp.int32)
    col_valid = (k_cols[None, :] >= q_cols[:, None]) & (k_cols[None, :] <= q_cols[:, None] + 2 * radius)
    allowed = row_valid[:, None, :, None] & col_valid[None, :, None, :]
    return allowed.reshape(query_rows * query_cols, key_rows * key_cols)

def tile_terms(queries, keys, values, grad_heads, window, head_count):
    q_count, model_width = queries.shape
    k_count = keys.shape[0]
    head_dim = model_width // head_count
    softmax_scale = 1.0 / math.sqrt(head_dim)
    query_f = queries.reshape(q_count, head_count, head_dim).astype(jnp.float32)
    key_f = keys.reshape(k_count, head_count, head_dim).astype(jnp.float32)
    value_f = values.reshape(k_count, head_count, head_dim).astype(jnp.float32)
    grad_f = grad_heads.reshape(q_count, head_count, head_dim).astype(jnp.float32)
    scores = jnp.einsum('qhe,khe->hqk', query_f, key_f) * softmax_scale
    scores = jnp.where(window[None], scores, -jnp.inf)
    row_max = lax.optimization_barrier(jnp.max(scores, axis=2, keepdims=True))
    exp_terms = jnp.exp(scores - row_max)
    prob_f32 = exp_terms / lax.optimization_barrier(jnp.sum(exp_terms, axis=2, keepdims=True))
    prob_b16 = prob_f32.astype(jnp.bfloat16)
    attended = jnp.einsum('hqk,khe->qhe', prob_b16.astype(jnp.float32), value_f).astype(jnp.bfloat16)
    row_term = lax.optimization_barrier(jnp.sum(grad_f * attended.astype(jnp.float32), axis=2))
    dprob = jnp.einsum('qhe,khe->hqk', grad_f, value_f)
    dscore = (prob_f32 * (dprob - row_term.T[:, :, None])).astype(jnp.bfloat16).astype(jnp.float32)
    grad_query = jnp.einsum('hqk,khe->qhe', dscore, key_f).reshape(q_count, model_width)
    grad_key = jnp.einsum('hqk,qhe->khe', dscore, query_f).reshape(k_count, model_width)
    grad_value = jnp.einsum('hqk,qhe->khe', prob_b16.astype(jnp.float32), grad_f).reshape(k_count, model_width)
    return (attended.reshape(q_count, model_width), grad_query, grad_key, grad_value)

def reference(features, grad_output, qkv_weight, out_weight):
    model_width = features.shape[2]
    radius = RADIUS
    x_rows = features.reshape(-1, model_width)
    grad_rows = grad_output.reshape(-1, model_width)
    projected = jnp.dot(x_rows, qkv_weight, preferred_element_type=jnp.float32).astype(jnp.bfloat16)
    projected = projected.reshape(NLAT, NLON, 3 * model_width)
    grad_attn = jnp.dot(grad_rows, out_weight.T, preferred_element_type=jnp.float32).astype(jnp.bfloat16)
    grad_attn = grad_attn.reshape(NLAT, NLON, model_width)
    queries = projected[..., :model_width]
    key_value = projected[..., model_width:]
    wrapped = jnp.concatenate([key_value[:, NLON - radius:], key_value, key_value[:, :radius]], axis=1)
    padded = jnp.pad(wrapped, ((radius, radius), (0, 0), (0, 0)))
    tiles_lon = NLON // QCOLS
    tile_count = NLAT // QROWS * tiles_lon
    key_rows = QROWS + 2 * radius
    key_cols = QCOLS + 2 * radius
    zero_index = jnp.int32(0)

    def tile_step(tile_index, state_tuple):
        out_all, query_all, grad_acc = state_tuple
        tile_lat = (tile_index // tiles_lon).astype(jnp.int32)
        tile_lon = (tile_index % tiles_lon).astype(jnp.int32)
        first_row = (tile_lat * QROWS).astype(jnp.int32)
        first_col = (tile_lon * QCOLS).astype(jnp.int32)
        q_tile = lax.dynamic_slice(queries, (first_row, first_col, zero_index), (QROWS, QCOLS, model_width)).reshape(-1, model_width)
        g_tile = lax.dynamic_slice(grad_attn, (first_row, first_col, zero_index), (QROWS, QCOLS, model_width)).reshape(-1, model_width)
        kv_tile = lax.dynamic_slice(padded, (first_row, first_col, zero_index), (key_rows, key_cols, 2 * model_width)).reshape(-1, 2 * model_width)
        window = window_mask(first_row, QROWS, QCOLS, key_rows, key_cols, radius, NLAT)
        attended, grad_query, grad_key, grad_value = tile_terms(q_tile, kv_tile[:, :model_width], kv_tile[:, model_width:], g_tile, window, HEADS)
        out_all = lax.dynamic_update_slice(out_all, attended.reshape(QROWS, QCOLS, model_width), (first_row, first_col, zero_index))
        query_all = lax.dynamic_update_slice(query_all, grad_query.reshape(QROWS, QCOLS, model_width), (first_row, first_col, zero_index))
        region = lax.dynamic_slice(grad_acc, (first_row, first_col, zero_index), (key_rows, key_cols, 2 * model_width))
        region = region + jnp.concatenate([grad_key, grad_value], axis=1).reshape(key_rows, key_cols, 2 * model_width)
        grad_acc = lax.dynamic_update_slice(grad_acc, region, (first_row, first_col, zero_index))
        return (out_all, query_all, grad_acc)
    start_state = (jnp.zeros((NLAT, NLON, model_width), jnp.bfloat16), jnp.zeros((NLAT, NLON, model_width), jnp.float32), jnp.zeros((NLAT + 2 * radius, NLON + 2 * radius, 2 * model_width), jnp.float32))
    out_all, query_all, grad_acc = lax.fori_loop(jnp.int32(0), jnp.int32(tile_count), tile_step, start_state)
    interior = grad_acc[radius:radius + NLAT]
    middle = interior[:, radius:radius + NLON]
    middle = middle.at[:, :radius].add(interior[:, radius + NLON:])
    middle = middle.at[:, NLON - radius:].add(interior[:, :radius])
    softmax_scale = 1.0 / math.sqrt(model_width // HEADS)
    grad_query = (query_all * softmax_scale).astype(jnp.bfloat16).reshape(-1, model_width)
    grad_key = (middle[..., :model_width] * softmax_scale).astype(jnp.bfloat16).reshape(-1, model_width)
    grad_value = middle[..., model_width:].astype(jnp.bfloat16).reshape(-1, model_width)
    grad_proj = jnp.concatenate([grad_query, grad_key, grad_value], axis=1)
    grad_features = jnp.dot(grad_proj, qkv_weight.T, preferred_element_type=jnp.float32).astype(jnp.bfloat16)
    grad_qkv = jnp.dot(x_rows.T, grad_proj, preferred_element_type=jnp.float32)
    grad_out = jnp.dot(out_all.reshape(-1, model_width).T, grad_rows, preferred_element_type=jnp.float32)
    return (grad_features.reshape(NLAT, NLON, model_width), grad_qkv, grad_out)
```

```python
import functools
import math

import jax
import jax.numpy as jnp
from jax import lax
from jax.experimental import pallas as pl
from jax.experimental.pallas import tpu as pltpu
from jax.sharding import PartitionSpec as P

MESH = pl.DeviceIdType.MESH
BF = jnp.bfloat16
F32 = jnp.float32


def place():
    lat = lax.axis_index("lat")
    lon = lax.axis_index("lon")
    z, x_lo = lat // 2, lat % 2
    y, x_hi, core = lon // 4, (lon // 2) % 2, lon % 2
    return {"z": z, "y": y, "x": x_hi * 2 + x_lo}, core


def device(at, core):
    return (at["z"] * 2 + at["x"] % 2, at["y"] * 4 + (at["x"] // 2) * 2 + core)


def moved(at, axis, steps):
    out = dict(at)
    out[axis] = (at[axis] + steps + 4) % 4
    return out


def meet(peers):
    barrier = pltpu.get_barrier_semaphore()
    for peer in peers:
        pl.semaphore_signal(barrier, inc=1, device_id=peer, device_id_type=MESH)
    pl.semaphore_wait(barrier, len(peers))


def torus_peers(at, core):
    peers = [device(at, 1 - core)]
    for axis in ("z", "y", "x"):
        for steps in (1, -1):
            peers.append(device(moved(at, axis, steps), core))
    return peers


ORDERS = (("x", "y", "z"), ("y", "z", "x"), ("z", "x", "y"))


def region(at, full, axis=None, coord=None):
    index = []
    for name in ("z", "y", "x"):
        if name == axis:
            index.append(coord)
        elif name in full:
            index.append(slice(None))
        else:
            index.append(at[name])
    return tuple(index)


def send(src, dst, ssem, rsem, peer):
    copy = pltpu.make_async_remote_copy(
        src_ref=src, dst_ref=dst, send_sem=ssem, recv_sem=rsem, device_id=peer, device_id_type=MESH
    )
    copy.start()
    return copy


def unpack(blocks, write):
    def body(step, carry):
        z, rest = step // 4, step % 4
        x_lo, y_pair = rest // 2, rest % 2
        for part in range(3):
            for parity in range(2):
                pieces = []
                for y in range(2):
                    for x_hi in range(2):
                        for core in range(2):
                            piece = blocks[part, parity, z, 2 * y_pair + y, 2 * x_hi + x_lo, core]
                            pieces.append(piece.astype(F32).reshape(24, 128))
                for chunk in range(4):
                    rows = jnp.concatenate([p[6 * chunk : 6 * chunk + 6] for p in pieces], axis=0)
                    write(step, 8 * part + 4 * parity + chunk, rows.astype(BF))
        return carry

    lax.fori_loop(0, 16, body, 0)


def gather(own):
    def kernel(own_ref, qkv_ref, out_ref, blocks, ssem, rsem, psem, local_sem):
        at, core = place()
        meet(torus_peers(at, core))
        partner = device(at, 1 - core)
        z, y, x = at["z"], at["y"], at["x"]
        local = pltpu.make_async_copy(own_ref.at[:, core], blocks.at[:, core, z, y, x, core], local_sem)
        local.start()
        pair = send(
            own_ref.at[:, 1 - core], blocks.at[:, 1 - core, z, y, x, core], psem.at[0, 0], psem.at[1, 0], partner
        )
        local.wait()
        pair.wait_recv()
        sent = [pair]
        lasts = []
        for stage in range(3):
            whole, rounds = {}, {}
            for part in range(3):
                axis, full = ORDERS[part][stage], ORDERS[part][:stage]
                for k, steps in ((0, 1), (1, -1)):
                    where = (part, core) + region(at, full, axis, at[axis])
                    whole[part, k] = send(
                        blocks.at[where], blocks.at[where], ssem.at[part, stage, k], rsem.at[part, stage, k],
                        device(moved(at, axis, steps), core),
                    )
            for part in range(3):
                axis, full = ORDERS[part][stage], ORDERS[part][:stage]
                for k, steps in ((0, 1), (1, -1)):
                    whole[part, k].wait_recv()
                    back = (at[axis] - steps + 4) % 4
                    where = (part, core) + region(at, full, axis, back) + (k,)
                    rounds[part, k] = send(
                        blocks.at[where], blocks.at[where], ssem.at[part, stage, 2 + k],
                        rsem.at[part, stage, 2 + k], device(moved(at, axis, steps), core),
                    )
            for part in range(3):
                for k in range(2):
                    rounds[part, k].wait_recv()
                    sent += [whole[part, k], rounds[part, k]]
                if stage == 2:
                    lasts.append(
                        send(
                            blocks.at[part, core], blocks.at[part, core], psem.at[0, 1 + part],
                            psem.at[1, 1 + part], partner,
                        )
                    )
        for copy in lasts:
            copy.wait_recv()
        for copy in sent + lasts:
            copy.wait_send()

        def write(step, chunk, rows):
            first = pl.multiple_of(step * 48, 16)
            if chunk < 18:
                qkv_ref[pl.ds(first, 48), 128 * chunk : 128 * chunk + 128] = rows
            else:
                chunk -= 18
                out_ref[pl.ds(first, 48), 128 * chunk : 128 * chunk + 128] = rows

        unpack(blocks, write)

    vmem = pl.BlockSpec(memory_space=pltpu.VMEM)
    return pl.pallas_call(
        kernel,
        out_shape=(jax.ShapeDtypeStruct((768, 2304), BF), jax.ShapeDtypeStruct((768, 768), BF)),
        in_specs=[vmem],
        out_specs=(vmem, vmem),
        scratch_shapes=[
            pltpu.VMEM((3, 2, 4, 4, 4, 2, 3, 8, 128), BF),
            pltpu.SemaphoreType.DMA((3, 3, 4)),
            pltpu.SemaphoreType.DMA((3, 3, 4)),
            pltpu.SemaphoreType.DMA((2, 4)),
            pltpu.SemaphoreType.DMA,
        ],
        compiler_params=pltpu.CompilerParams(collective_id=0, has_side_effects=True),
        name="gather_weights",
    )(own)


def to_blocks(qkv, out):
    rows = jnp.concatenate([qkv, out], axis=1)
    rows = rows.reshape(6, 6, 4, 128).transpose(1, 2, 0, 3)
    return rows.reshape(3, 2, 3, 8, 128)


def from_blocks(blocks):
    rows = blocks.reshape(6, 4, 6, 128).transpose(2, 0, 1, 3)
    return rows.reshape(6, 3072)


def scatter(first, second):
    def kernel(
        qkv_ref, out_ref, own_ref, blocks, pair_in, half0, whole0, half1, whole1, half2, whole2, last_out, last_in,
        ssem, rsem, psem,
    ):
        at, core = place()
        meet(torus_peers(at, core))
        partner = device(at, 1 - core)
        halves, wholes = (half0, half1, half2), (whole0, whole1, whole2)
        sent = []

        def pack(part):
            def body(step, carry):
                z, rest = step // 4, step % 4
                x_lo, y_pair = rest // 2, rest % 2
                first_row = pl.multiple_of(step * 48, 16)
                for parity in range(2):
                    chunks = []
                    for q in range(4):
                        c = 8 * part + 4 * parity + q
                        ref, c = (qkv_ref, c) if c < 18 else (out_ref, c - 18)
                        chunks.append(ref[pl.ds(first_row, 48), 128 * c : 128 * c + 128].astype(F32))
                    for e in range(8):
                        y, x_hi, to = e // 4, (e // 2) % 2, e % 2
                        rows = jnp.concatenate([c[6 * e : 6 * e + 6] for c in chunks], axis=0)
                        blocks[part, parity, z, 2 * y_pair + y, 2 * x_hi + x_lo, to] = rows.reshape(3, 8, 128).astype(BF)
                return carry

            lax.fori_loop(0, 16, body, 0)

        pairs = []
        for part in range(3):
            pack(part)
            pairs.append(
                send(blocks.at[part, 1 - core], pair_in.at[part], psem.at[0, part], psem.at[1, part], partner)
            )
        sent += pairs
        for part in range(3):
            pairs[part].wait_recv()

            def add(step, carry, part=part):
                z, rest = step // 16, step % 16
                y, x = rest // 4, rest % 4
                total = blocks[part, core, z, y, x].astype(F32) + pair_in[part, z, y, x].astype(F32)
                blocks[part, core, z, y, x] = total.astype(BF)
                return carry

            lax.fori_loop(0, 64, add, 0)

        def each(full, body):
            count = len(full)
            if count == 0:
                body(())
            elif count == 1:
                lax.fori_loop(0, 4, lambda i, c: (body((i,)), c)[1], 0)
            else:
                lax.fori_loop(0, 16, lambda i, c: (body((i // 4, i % 4)), c)[1], 0)

        def spot(part, where, inner):
            inner = list(inner)
            return (part, core) + tuple(inner.pop(0) if isinstance(w, slice) else w for w in where)

        for stage in range(3):
            early, late = {}, {}
            plan = {}
            for part in range(3):
                order = ORDERS[part][::-1]
                axis, full = order[stage], order[stage + 1 :]
                plan[part] = (axis, full)
                far = region(at, full, axis, (at[axis] + 2) % 4)
                for k, steps in ((0, 1), (1, -1)):
                    early[part, k] = send(
                        blocks.at[(part, core) + far + (k,)], halves[stage].at[part, k],
                        ssem.at[part, stage, k], rsem.at[part, stage, k], device(moved(at, axis, steps), core),
                    )
            for part in range(3):
                axis, full = plan[part]
                for k, steps in ((0, 1), (1, -1)):
                    early[part, k].wait_recv()
                    near = region(at, full, axis, (at[axis] + steps + 4) % 4)

                    def add(inner, part=part, k=k, near=near):
                        here = spot(part, near, inner) + (k,)
                        total = blocks[here].astype(F32) + halves[stage][(part, k) + inner].astype(F32)
                        blocks[here] = total.astype(BF)

                    each(full, add)
                    late[part, k] = send(
                        blocks.at[(part, core) + near], wholes[stage].at[part, k],
                        ssem.at[part, stage, 2 + k], rsem.at[part, stage, 2 + k], device(moved(at, axis, steps), core),
                    )
            for part in range(3):
                axis, full = plan[part]
                late[part, 0].wait_recv()
                late[part, 1].wait_recv()
                mine = region(at, full, axis, at[axis])

                def add(inner, part=part, mine=mine):
                    here = spot(part, mine, inner)
                    total = blocks[here].astype(F32) + wholes[stage][(part, 0) + inner].astype(F32)
                    total = total + wholes[stage][(part, 1) + inner].astype(F32)
                    if stage < 2:
                        blocks[here] = total.astype(BF)
                    else:
                        last_out[part] = total

                each(full, add)
                sent += [early[part, 0], early[part, 1], late[part, 0], late[part, 1]]
        ends = []
        for part in range(3):
            ends.append(
                send(last_out.at[part, 1 - core], last_in.at[part], psem.at[0, 3 + part], psem.at[1, 3 + part], partner)
            )
        for part in range(3):
            own_ref[part, core] = last_out[part, core]
        for part in range(3):
            ends[part].wait_recv()
            own_ref[part, 1 - core] = last_in[part]
        for copy in sent + ends:
            copy.wait_send()

    vmem = pl.BlockSpec(memory_space=pltpu.VMEM)
    tail = (3, 8, 128)
    own = pl.pallas_call(
        kernel,
        out_shape=jax.ShapeDtypeStruct((3, 2) + tail, F32),
        in_specs=[vmem, vmem],
        out_specs=vmem,
        scratch_shapes=[
            pltpu.VMEM((3, 2, 4, 4, 4, 2) + tail, BF),
            pltpu.VMEM((3, 4, 4, 4, 2) + tail, BF),
            pltpu.VMEM((3, 2, 4, 4) + tail, BF),
            pltpu.VMEM((3, 2, 4, 4, 2) + tail, BF),
            pltpu.VMEM((3, 2, 4) + tail, BF),
            pltpu.VMEM((3, 2, 4, 2) + tail, BF),
            pltpu.VMEM((3, 2) + tail, BF),
            pltpu.VMEM((3, 2, 2) + tail, BF),
            pltpu.VMEM((3, 2) + tail, F32),
            pltpu.VMEM((3,) + tail, F32),
            pltpu.SemaphoreType.DMA((3, 3, 4)),
            pltpu.SemaphoreType.DMA((3, 3, 4)),
            pltpu.SemaphoreType.DMA((2, 6)),
        ],
        compiler_params=pltpu.CompilerParams(collective_id=1, has_side_effects=True, vmem_limit_bytes=60 << 20),
        name="scatter_grads",
    )(first, second)
    return from_blocks(own)

HEADS = 12
RADIUS = 6
QROWS = 16
QCOLS = 16


heads_together = 2


def shifted(value, axis, steps):
    count = lax.axis_size(axis)
    pairs = [(source, (source + steps) % count) for source in range(count)]
    return lax.ppermute(value, axis, pairs)


def shifted_2(value, axis, steps):
    count = lax.axis_size(axis)
    leading, last = (max(0, -steps), min(count, count - steps))
    return lax.ppermute(value, axis, [(source, source + steps) for source in range(leading, last)])


def padded(array, sides, width, wrap):
    for axis, dim in sides:
        devices, length = (lax.axis_size(axis), array.shape[dim])
        up = [(i, (i + 1) % devices) for i in range(devices if wrap else devices - 1)]
        down = [(j, i) for i, j in up]
        last = lax.slice_in_dim(array, length - width, length, axis=dim)
        leading = lax.slice_in_dim(array, 0, width, axis=dim)
        before = lax.ppermute(last, axis, up)
        after = lax.ppermute(leading, axis, down)
        array = jnp.concatenate([before, array, after], axis=dim)
    return array


def window_mask(row_first, query_rows, query_cols, key_rows, key_cols, radius, total_rows):
    q_rows = row_first + jnp.arange(query_rows, dtype=jnp.int32)
    k_rows = row_first - radius + jnp.arange(key_rows, dtype=jnp.int32)
    row_start = jnp.clip(q_rows - radius, 0, total_rows - 2 * radius - 1)
    row_valid = (k_rows[None, :] >= row_start[:, None]) & (
        k_rows[None, :] <= row_start[:, None] + 2 * radius
    )
    q_cols = jnp.arange(query_cols, dtype=jnp.int32)
    k_cols = jnp.arange(key_cols, dtype=jnp.int32)
    col_valid = (k_cols[None, :] >= q_cols[:, None]) & (
        k_cols[None, :] <= q_cols[:, None] + 2 * radius
    )
    allowed = row_valid[:, None, :, None] & col_valid[None, :, None, :]
    return allowed.reshape(query_rows * query_cols, key_rows * key_cols)


def tile_terms(queries, keys, values, grad_heads, window, head_count, head_dim):
    q_count = queries.shape[0]
    k_count = keys.shape[0]
    softmax_scale = 1.0 / math.sqrt(head_dim)
    query_h = queries.reshape(q_count, head_count, head_dim)
    key_h = keys.reshape(k_count, head_count, head_dim)
    value_h = values.reshape(k_count, head_count, head_dim)
    grad_h = grad_heads.reshape(q_count, head_count, head_dim)
    scores = (
        jnp.einsum("qhe,khe->hqk", query_h, key_h, preferred_element_type=jnp.float32)
        * softmax_scale
    )
    scores = jnp.where(window[None], scores, -jnp.inf)
    row_max = jnp.max(scores, axis=2, keepdims=True)
    exp_terms = jnp.exp(scores - row_max)
    prob_f32 = exp_terms / jnp.sum(exp_terms, axis=2, keepdims=True)
    prob_b16 = prob_f32.astype(jnp.bfloat16)
    attended = jnp.einsum(
        "hqk,khe->qhe", prob_b16, value_h, preferred_element_type=jnp.float32
    ).astype(jnp.bfloat16)
    row_term = jnp.sum(grad_h.astype(jnp.float32) * attended.astype(jnp.float32), axis=2)
    dprob = jnp.einsum("qhe,khe->hqk", grad_h, value_h, preferred_element_type=jnp.float32)
    dscore = (prob_f32 * (dprob - row_term.T[:, :, None])).astype(jnp.bfloat16)
    grad_query = jnp.einsum("hqk,khe->qhe", dscore, key_h, preferred_element_type=jnp.float32)
    grad_key = jnp.einsum("hqk,qhe->khe", dscore, query_h, preferred_element_type=jnp.float32)
    grad_value = jnp.einsum("hqk,qhe->khe", prob_b16, grad_h, preferred_element_type=jnp.float32)
    model_part = head_count * head_dim
    return (
        attended.reshape(q_count, model_part),
        grad_query.reshape(q_count, model_part),
        grad_key.reshape(k_count, model_part),
        grad_value.reshape(k_count, model_part),
    )


def turn_lon(strip_part, offset):
    return shifted(strip_part.astype(jnp.bfloat16), "lon", offset).astype(strip_part.dtype)


def turn_lat(strip_part, offset):
    return shifted_2(strip_part.astype(jnp.bfloat16), "lat", offset).astype(strip_part.dtype)


def shards(features, grad_output, qkv_weight, out_weight):
    lat_rows, lon_cols, model_width = features.shape
    radius = RADIUS
    head_dim = model_width // HEADS
    qkv_full, out_full = gather(to_blocks(qkv_weight, out_weight))
    x_rows = features.reshape(-1, model_width)
    grad_rows = grad_output.reshape(-1, model_width)
    projected = jnp.dot(x_rows, qkv_full, preferred_element_type=jnp.float32).astype(jnp.bfloat16)
    projected = projected.reshape(lat_rows, lon_cols, 3 * model_width)
    grad_attn = lax.dot_general(
        grad_rows, out_full, (((1,), (1,)), ((), ())), preferred_element_type=jnp.float32
    )
    grad_attn = grad_attn.astype(jnp.bfloat16).reshape(lat_rows, lon_cols, model_width)
    queries = projected[..., :model_width]
    key_value = projected[..., model_width:]
    lon_wide = padded(key_value, (("lon", 1),), radius, True)
    extended = padded(lon_wide, (("lat", 0),), radius, False)
    total_rows = lat_rows * lax.axis_size("lat")
    lat_first = lax.axis_index("lat") * lat_rows
    key_rows = QROWS + 2 * radius
    key_cols = QCOLS + 2 * radius
    wide_cols = lon_cols + 2 * radius
    grad_kv = jnp.zeros((lat_rows + 2 * radius, wide_cols, 2 * model_width), jnp.float32)
    window = window_mask(lat_first + 0, QROWS, QCOLS, key_rows, key_cols, radius, total_rows)
    out_row = []
    query_row = []
    for col_index in range(lon_cols // QCOLS):
        left_col = col_index * QCOLS
        q_tile = queries[0:QROWS, left_col : left_col + QCOLS].reshape(-1, model_width)
        g_tile = grad_attn[0:QROWS, left_col : left_col + QCOLS].reshape(-1, model_width)
        kv_tile = extended[0:key_rows, left_col : left_col + key_cols].reshape(-1, 2 * model_width)
        out_parts, query_parts, key_parts, value_parts = ([], [], [], [])
        for first_head in range(0, HEADS, heads_together):
            col_low = first_head * head_dim
            col_high = col_low + heads_together * head_dim
            attended, grad_query, grad_key, grad_value = tile_terms(
                q_tile[:, col_low:col_high],
                kv_tile[:, col_low:col_high],
                kv_tile[:, model_width + col_low : model_width + col_high],
                g_tile[:, col_low:col_high],
                window,
                heads_together,
                head_dim,
            )
            out_parts.append(attended)
            query_parts.append(grad_query)
            key_parts.append(grad_key)
            value_parts.append(grad_value)
        out_row.append(jnp.concatenate(out_parts, axis=1).reshape(QROWS, QCOLS, model_width))
        query_row.append(jnp.concatenate(query_parts, axis=1).reshape(QROWS, QCOLS, model_width))
        key_part = jnp.concatenate(key_parts + value_parts, axis=1).reshape(
            key_rows, key_cols, 2 * model_width
        )
        grad_kv = grad_kv.at[0:key_rows, left_col : left_col + key_cols].add(key_part)
    out_blocks = jnp.concatenate(out_row, axis=1)
    query_blocks = jnp.concatenate(query_row, axis=1)
    from_right = turn_lon(grad_kv[:, :radius], -1)
    from_left = turn_lon(grad_kv[:, wide_cols - radius :], 1)
    middle = grad_kv[:, radius : radius + lon_cols]
    middle = middle.at[:, :radius].add(from_left)
    middle = middle.at[:, lon_cols - radius :].add(from_right)
    from_below = turn_lat(middle[:radius], -1)
    from_above = turn_lat(middle[lat_rows + radius :], 1)
    interior = middle[radius : radius + lat_rows]
    interior = interior.at[:radius].add(from_above)
    interior = interior.at[lat_rows - radius :].add(from_below)
    softmax_scale = 1.0 / math.sqrt(head_dim)
    query_all = query_blocks.reshape(-1, model_width)
    grad_query = (query_all * softmax_scale).astype(jnp.bfloat16)
    grad_key = (
        (interior[..., :model_width] * softmax_scale).astype(jnp.bfloat16).reshape(-1, model_width)
    )
    grad_value = interior[..., model_width:].astype(jnp.bfloat16).reshape(-1, model_width)
    grad_proj = jnp.concatenate([grad_query, grad_key, grad_value], axis=1)
    attended_rows = out_blocks.reshape(-1, model_width)
    grad_features = lax.dot_general(
        grad_proj, qkv_full, (((1,), (1,)), ((), ())), preferred_element_type=jnp.float32
    )
    grad_features = grad_features.astype(jnp.bfloat16).reshape(lat_rows, lon_cols, model_width)
    first_term = lax.dot_general(
        x_rows, grad_proj, (((0,), (0,)), ((), ())), preferred_element_type=jnp.float32
    )
    second_term = lax.dot_general(
        attended_rows, grad_rows, (((0,), (0,)), ((), ())), preferred_element_type=jnp.float32
    )
    my_grads = scatter(first_term, second_term)
    return (grad_features, my_grads[:, : 3 * model_width], my_grads[:, 3 * model_width :])


def solution(mesh):
    placed = (
        P("lat", "lon", None),
        P("lat", "lon", None),
        P(("lat", "lon"), None),
        P(("lat", "lon"), None),
    )
    return jax.shard_map(
        shards,
        mesh=mesh,
        in_specs=placed,
        out_specs=(P("lat", "lon", None), P(("lat", "lon"), None), P(("lat", "lon"), None)),
        check_vma=False,
    )
```

```python
import functools
import math

import jax
import jax.numpy as jnp
from jax import lax
from jax.experimental import pallas as pl
from jax.experimental.pallas import tpu as pltpu
from jax.sharding import PartitionSpec as P

MESH = pl.DeviceIdType.MESH
BF = jnp.bfloat16
F32 = jnp.float32


def place():
    lat = lax.axis_index("lat")
    lon = lax.axis_index("lon")
    z, x_lo = lat // 2, lat % 2
    y, x_hi, core = lon // 4, (lon // 2) % 2, lon % 2
    return {"z": z, "y": y, "x": x_hi * 2 + x_lo}, core


def device(at, core):
    return (at["z"] * 2 + at["x"] % 2, at["y"] * 4 + (at["x"] // 2) * 2 + core)


def moved(at, axis, steps):
    out = dict(at)
    out[axis] = (at[axis] + steps + 4) % 4
    return out


def meet(peers):
    barrier = pltpu.get_barrier_semaphore()
    for peer in peers:
        pl.semaphore_signal(barrier, inc=1, device_id=peer, device_id_type=MESH)
    pl.semaphore_wait(barrier, len(peers))


def torus_peers(at, core):
    peers = [device(at, 1 - core)]
    for axis in ("z", "y", "x"):
        for steps in (1, -1):
            peers.append(device(moved(at, axis, steps), core))
    return peers


ORDERS = (("x", "y", "z"), ("y", "z", "x"), ("z", "x", "y"))


def region(at, full, axis=None, coord=None):
    index = []
    for name in ("z", "y", "x"):
        if name == axis:
            index.append(coord)
        elif name in full:
            index.append(slice(None))
        else:
            index.append(at[name])
    return tuple(index)


def send(src, dst, ssem, rsem, peer):
    copy = pltpu.make_async_remote_copy(
        src_ref=src, dst_ref=dst, send_sem=ssem, recv_sem=rsem, device_id=peer, device_id_type=MESH
    )
    copy.start()
    return copy


def unpack(blocks, write):
    def body(step, carry):
        z, rest = step // 4, step % 4
        x_lo, y_pair = rest // 2, rest % 2
        for part in range(3):
            for parity in range(2):
                pieces = []
                for y in range(2):
                    for x_hi in range(2):
                        for core in range(2):
                            piece = blocks[part, parity, z, 2 * y_pair + y, 2 * x_hi + x_lo, core]
                            pieces.append(piece.astype(F32).reshape(24, 128))
                for chunk in range(4):
                    rows = jnp.concatenate([p[6 * chunk : 6 * chunk + 6] for p in pieces], axis=0)
                    write(step, 8 * part + 4 * parity + chunk, rows.astype(BF))
        return carry

    lax.fori_loop(0, 16, body, 0)


def gather(own, features):
    def kernel(own_ref, x_ref, qkv_ref, out_ref, ext_ref, blocks, ssem, rsem, psem, local_sem, hssem, hrsem):
        at, core = place()
        meet(torus_peers(at, core) + neighbours())
        partner = device(at, 1 - core)
        z, y, x = at["z"], at["y"], at["x"]
        local = pltpu.make_async_copy(own_ref.at[:, core], blocks.at[:, core, z, y, x, core], local_sem)
        local.start()
        inner = pltpu.make_async_copy(x_ref, ext_ref.at[6:22, 8:40], hssem.at[8])
        inner.start()
        pair = send(
            own_ref.at[:, 1 - core], blocks.at[:, 1 - core, z, y, x, core], psem.at[0, 0], psem.at[1, 0], partner
        )
        local.wait()
        pair.wait_recv()
        sent = [pair]
        lasts = []
        halos = []
        for side, (row_step, col_step) in enumerate(SIDES):
            src = x_ref.at[cut(OWN_ROWS, row_step), cut(OWN_COLS, col_step)]
            dst = ext_ref.at[cut(HALO_ROWS, -row_step), cut(HALO_COLS, -col_step)]
            halos.append(send(src, dst, hssem.at[side], hrsem.at[side], beside(row_step, col_step)))
        for stage in range(3):
            whole, rounds = {}, {}
            for part in range(3):
                axis, full = ORDERS[part][stage], ORDERS[part][:stage]
                for k, steps in ((0, 1), (1, -1)):
                    where = (part, core) + region(at, full, axis, at[axis])
                    whole[part, k] = send(
                        blocks.at[where], blocks.at[where], ssem.at[part, stage, k], rsem.at[part, stage, k],
                        device(moved(at, axis, steps), core),
                    )
            for part in range(3):
                axis, full = ORDERS[part][stage], ORDERS[part][:stage]
                for k, steps in ((0, 1), (1, -1)):
                    whole[part, k].wait_recv()
                    back = (at[axis] - steps + 4) % 4
                    where = (part, core) + region(at, full, axis, back) + (k,)
                    rounds[part, k] = send(
                        blocks.at[where], blocks.at[where], ssem.at[part, stage, 2 + k],
                        rsem.at[part, stage, 2 + k], device(moved(at, axis, steps), core),
                    )
            for part in range(3):
                for k in range(2):
                    rounds[part, k].wait_recv()
                    sent += [whole[part, k], rounds[part, k]]
                if stage == 2:
                    lasts.append(
                        send(
                            blocks.at[part, core], blocks.at[part, core], psem.at[0, 1 + part],
                            psem.at[1, 1 + part], partner,
                        )
                    )
        for copy in lasts:
            copy.wait_recv()
        for copy in sent + lasts:
            copy.wait_send()

        def write(step, chunk, rows):
            first = pl.multiple_of(step * 48, 16)
            if chunk < 18:
                qkv_ref[pl.ds(first, 48), 128 * chunk : 128 * chunk + 128] = rows
            else:
                chunk -= 18
                out_ref[pl.ds(first, 48), 128 * chunk : 128 * chunk + 128] = rows

        unpack(blocks, write)
        for copy in halos:
            copy.wait_recv()
        for copy in halos:
            copy.wait_send()
        inner.wait()

    vmem = pl.BlockSpec(memory_space=pltpu.VMEM)
    return pl.pallas_call(
        kernel,
        out_shape=(
            jax.ShapeDtypeStruct((768, 2304), BF),
            jax.ShapeDtypeStruct((768, 768), BF),
            jax.ShapeDtypeStruct((28, 48, 768), BF),
        ),
        in_specs=[vmem, vmem],
        out_specs=(vmem, vmem, vmem),
        scratch_shapes=[
            pltpu.VMEM((3, 2, 4, 4, 4, 2, 3, 8, 128), BF),
            pltpu.SemaphoreType.DMA((3, 3, 4)),
            pltpu.SemaphoreType.DMA((3, 3, 4)),
            pltpu.SemaphoreType.DMA((2, 4)),
            pltpu.SemaphoreType.DMA,
            pltpu.SemaphoreType.DMA((9,)),
            pltpu.SemaphoreType.DMA((8,)),
        ],
        compiler_params=pltpu.CompilerParams(collective_id=0, has_side_effects=True),
        name="gather_weights",
    )(own, features)


def to_blocks(qkv, out):
    rows = jnp.concatenate([qkv, out], axis=1)
    rows = rows.reshape(6, 6, 4, 128).transpose(1, 2, 0, 3)
    return rows.reshape(3, 2, 3, 8, 128)


def from_blocks(blocks):
    rows = blocks.reshape(6, 4, 6, 128).transpose(2, 0, 1, 3)
    return rows.reshape(6, 3072)


def scatter(first, second):
    def kernel(
        qkv_ref, out_ref, own_ref, blocks, pair_in, half0, whole0, half1, whole1, half2, whole2, last_out, last_in,
        ssem, rsem, psem,
    ):
        at, core = place()
        meet(torus_peers(at, core))
        partner = device(at, 1 - core)
        halves, wholes = (half0, half1, half2), (whole0, whole1, whole2)
        sent = []

        def pack(part):
            def body(step, carry):
                z, rest = step // 4, step % 4
                x_lo, y_pair = rest // 2, rest % 2
                first_row = pl.multiple_of(step * 48, 16)
                for parity in range(2):
                    chunks = []
                    for q in range(4):
                        c = 8 * part + 4 * parity + q
                        ref, c = (qkv_ref, c) if c < 18 else (out_ref, c - 18)
                        chunks.append(ref[pl.ds(first_row, 48), 128 * c : 128 * c + 128].astype(F32))
                    for e in range(8):
                        y, x_hi, to = e // 4, (e // 2) % 2, e % 2
                        rows = jnp.concatenate([c[6 * e : 6 * e + 6] for c in chunks], axis=0)
                        blocks[part, parity, z, 2 * y_pair + y, 2 * x_hi + x_lo, to] = rows.reshape(3, 8, 128).astype(BF)
                return carry

            lax.fori_loop(0, 16, body, 0)

        pairs = []
        for part in range(3):
            pack(part)
            pairs.append(
                send(blocks.at[part, 1 - core], pair_in.at[part], psem.at[0, part], psem.at[1, part], partner)
            )
        sent += pairs
        for part in range(3):
            pairs[part].wait_recv()

            def add(step, carry, part=part):
                z, rest = step // 16, step % 16
                y, x = rest // 4, rest % 4
                total = blocks[part, core, z, y, x].astype(F32) + pair_in[part, z, y, x].astype(F32)
                blocks[part, core, z, y, x] = total.astype(BF)
                return carry

            lax.fori_loop(0, 64, add, 0)

        def each(full, body):
            count = len(full)
            if count == 0:
                body(())
            elif count == 1:
                lax.fori_loop(0, 4, lambda i, c: (body((i,)), c)[1], 0)
            else:
                lax.fori_loop(0, 16, lambda i, c: (body((i // 4, i % 4)), c)[1], 0)

        def spot(part, where, inner):
            inner = list(inner)
            return (part, core) + tuple(inner.pop(0) if isinstance(w, slice) else w for w in where)

        for stage in range(3):
            early, late = {}, {}
            plan = {}
            for part in range(3):
                order = ORDERS[part][::-1]
                axis, full = order[stage], order[stage + 1 :]
                plan[part] = (axis, full)
                far = region(at, full, axis, (at[axis] + 2) % 4)
                for k, steps in ((0, 1), (1, -1)):
                    early[part, k] = send(
                        blocks.at[(part, core) + far + (k,)], halves[stage].at[part, k],
                        ssem.at[part, stage, k], rsem.at[part, stage, k], device(moved(at, axis, steps), core),
                    )
            for part in range(3):
                axis, full = plan[part]
                for k, steps in ((0, 1), (1, -1)):
                    early[part, k].wait_recv()
                    near = region(at, full, axis, (at[axis] + steps + 4) % 4)

                    def add(inner, part=part, k=k, near=near):
                        here = spot(part, near, inner) + (k,)
                        total = blocks[here].astype(F32) + halves[stage][(part, k) + inner].astype(F32)
                        blocks[here] = total.astype(BF)

                    each(full, add)
                    late[part, k] = send(
                        blocks.at[(part, core) + near], wholes[stage].at[part, k],
                        ssem.at[part, stage, 2 + k], rsem.at[part, stage, 2 + k], device(moved(at, axis, steps), core),
                    )
            for part in range(3):
                axis, full = plan[part]
                late[part, 0].wait_recv()
                late[part, 1].wait_recv()
                mine = region(at, full, axis, at[axis])

                def add(inner, part=part, mine=mine):
                    here = spot(part, mine, inner)
                    total = blocks[here].astype(F32) + wholes[stage][(part, 0) + inner].astype(F32)
                    total = total + wholes[stage][(part, 1) + inner].astype(F32)
                    if stage < 2:
                        blocks[here] = total.astype(BF)
                    else:
                        last_out[part] = total

                each(full, add)
                sent += [early[part, 0], early[part, 1], late[part, 0], late[part, 1]]
        ends = []
        for part in range(3):
            ends.append(
                send(last_out.at[part, 1 - core], last_in.at[part], psem.at[0, 3 + part], psem.at[1, 3 + part], partner)
            )
        for part in range(3):
            own_ref[part, core] = last_out[part, core]
        for part in range(3):
            ends[part].wait_recv()
            own_ref[part, 1 - core] = last_in[part]
        for copy in sent + ends:
            copy.wait_send()

    vmem = pl.BlockSpec(memory_space=pltpu.VMEM)
    tail = (3, 8, 128)
    own = pl.pallas_call(
        kernel,
        out_shape=jax.ShapeDtypeStruct((3, 2) + tail, F32),
        in_specs=[vmem, vmem],
        out_specs=vmem,
        scratch_shapes=[
            pltpu.VMEM((3, 2, 4, 4, 4, 2) + tail, BF),
            pltpu.VMEM((3, 4, 4, 4, 2) + tail, BF),
            pltpu.VMEM((3, 2, 4, 4) + tail, BF),
            pltpu.VMEM((3, 2, 4, 4, 2) + tail, BF),
            pltpu.VMEM((3, 2, 4) + tail, BF),
            pltpu.VMEM((3, 2, 4, 2) + tail, BF),
            pltpu.VMEM((3, 2) + tail, BF),
            pltpu.VMEM((3, 2, 2) + tail, BF),
            pltpu.VMEM((3, 2) + tail, F32),
            pltpu.VMEM((3,) + tail, F32),
            pltpu.SemaphoreType.DMA((3, 3, 4)),
            pltpu.SemaphoreType.DMA((3, 3, 4)),
            pltpu.SemaphoreType.DMA((2, 6)),
        ],
        compiler_params=pltpu.CompilerParams(collective_id=1, has_side_effects=True, vmem_limit_bytes=60 << 20),
        name="scatter_grads",
    )(first, second)
    return from_blocks(own)


RADIUS = 6
SIDES = ((-1, -1), (-1, 0), (-1, 1), (0, -1), (0, 1), (1, -1), (1, 0), (1, 1))
OWN_ROWS = {-1: (0, 6), 0: (0, 16), 1: (10, 6)}
OWN_COLS = {-1: (0, 8), 0: (0, 32), 1: (24, 8)}
HALO_ROWS = {-1: (0, 6), 0: (6, 16), 1: (22, 6)}
HALO_COLS = {-1: (0, 8), 0: (8, 32), 1: (40, 8)}


def cut(table, step):
    first, count = table[step]
    return slice(first, first + count)


def beside(row_step, col_step):
    lat = (lax.axis_index("lat") + row_step + 8) % 8
    lon = (lax.axis_index("lon") + col_step + 16) % 16
    return (lat, lon)


def neighbours():
    return [beside(a, b) for a, b in SIDES]


def window_bias(bias, start_of):
    lat = lax.axis_index("lat")
    shape = (32, 32, 128)

    def body(i, carry):
        group, part = i // 8, i % 8
        key_row = lat * 16 + start_of(group) - 6 + part * 2 + lax.broadcasted_iota(jnp.int32, (2, 32, 128), 0)
        key_col = lax.broadcasted_iota(jnp.int32, (2, 32, 128), 1)
        lane = lax.broadcasted_iota(jnp.int32, (2, 32, 128), 2) & 63
        query_row = lat * 16 + group * 4 + (lane >> 4)
        first = jnp.clip(query_row - RADIUS, 0, 128 - 2 * RADIUS - 1)
        apart = key_col - 8 - (lane & 15)
        good = (key_row >= first) & (key_row <= first + 2 * RADIUS) & (apart >= -RADIUS) & (apart <= RADIUS)
        bias[group, pl.ds(part * 64, 64)] = jnp.where(good, 0.0, -1e30).astype(F32).reshape(64, 128)
        return carry

    lax.fori_loop(0, 32, body, 0)


def dot(a, b, left, right):
    return lax.dot_general(a, b, (((left,), (right,)), ((), ())), preferred_element_type=F32)


def spread(rows):
    head = lax.broadcasted_iota(jnp.int32, (64, 256), 1) >> 6
    return jnp.concatenate([jnp.where(head == h, rows, 0) for h in range(4)], axis=0)


def gathered(full):
    head = lax.broadcasted_iota(jnp.int32, (64, 256), 1) >> 6
    out = full[0:64]
    for h in range(1, 4):
        out = jnp.where(head == h, full[64 * h : 64 * h + 64], out)
    return out


def attend(xext, grad_output, qkv_full, out_full):
    def kernel(
        x_ref, go_ref, wqkv_ref, wout_ref, att_ref, gp_ref, q, g, k, v, dk, dv, bias, out_s, out_c, out_r, in_s, in_c,
        in_r, ssem, rsem,
    ):
        lat = lax.axis_index("lat")
        low = jnp.where(lat == 0, 4, 0)
        high = jnp.where(lat == 7, 8, 12)

        def start_of(group):
            return jnp.clip(group * 4, low, high)

        meet(neighbours())
        window_bias(bias, start_of)

        def project_own(i, carry):
            rows = x_ref[pl.ds(6 + 4 * i, 4), 8:40].reshape(128, 768)
            grads = go_ref[pl.ds(4 * i, 4)].reshape(128, 768)
            for t in range(3):
                cols = slice(256 * t, 256 * t + 256)
                head = dot(rows, wqkv_ref[:, cols], 1, 0).astype(BF).astype(F32) * 0.125
                q[t, pl.ds(4 * i, 4)] = head.astype(BF).reshape(4, 32, 256)
                head = dot(grads, wout_ref[cols, :], 1, 1).astype(BF)
                g[t, pl.ds(4 * i, 4)] = head.reshape(4, 32, 256)
            return carry

        lax.fori_loop(0, 4, project_own, 0)

        def project_all(i, carry):
            rows = x_ref[pl.ds(4 * i, 4)].reshape(192, 768)
            for t in range(3):
                for ref, first in ((k, 768), (v, 1536)):
                    cols = slice(first + 256 * t, first + 256 * t + 256)
                    ref[t, pl.ds(4 * i, 4)] = dot(rows, wqkv_ref[:, cols], 1, 0).astype(BF).reshape(4, 48, 256)
            for t in range(3):
                dk[t, pl.ds(4 * i, 4)] = jnp.zeros((4, 48, 256), F32)
                dv[t, pl.ds(4 * i, 4)] = jnp.zeros((4, 48, 256), F32)
            return carry

        lax.fori_loop(0, 7, project_all, 0)

        def tile(i, carry):
            t, group = i // 4, i % 4
            start = start_of(group)
            lanes = pl.ds(pl.multiple_of(t * 256, 256), 256)
            mask = bias[group]
            mask = jnp.concatenate([mask, mask], axis=1)
            for j in range(2):
                q_cols, k_cols = slice(16 * j, 16 * j + 16), slice(16 * j, 16 * j + 32)
                q_b = spread(q[t, pl.ds(4 * group, 4), q_cols].reshape(64, 256))
                g_b = spread(g[t, pl.ds(4 * group, 4), q_cols].reshape(64, 256))
                k4 = k[t, pl.ds(start, 16), k_cols].reshape(512, 256)
                v4 = v[t, pl.ds(start, 16), k_cols].reshape(512, 256)
                scores = dot(k4, q_b, 1, 1) + mask
                top = jnp.max(scores, axis=0, keepdims=True)
                terms = jnp.exp(scores - top)
                probs = terms * (1.0 / jnp.sum(terms, axis=0, keepdims=True))
                probs_b = probs.astype(BF)
                att = gathered(dot(probs_b, v4, 0, 0)).astype(BF)
                att_ref[pl.ds(4 * group, 4), q_cols, lanes] = att.reshape(4, 16, 256)
                dprob = dot(v4, g_b, 1, 1)
                row_term = jnp.sum(probs * dprob, axis=0, keepdims=True)
                dscore = (probs * (dprob - row_term)).astype(BF)
                dq = gathered(dot(dscore, k4, 0, 0)) * 0.125
                gp_ref[pl.ds(4 * group, 4), q_cols, lanes] = dq.astype(BF).reshape(4, 16, 256)
                dk[t, pl.ds(start, 16), k_cols] += dot(dscore, q_b, 1, 0).reshape(16, 32, 256)
                dv[t, pl.ds(start, 16), k_cols] += dot(probs_b, g_b, 1, 0).reshape(16, 32, 256)
            return carry

        lax.fori_loop(0, 12, tile, 0)

        def slot(side, out):
            row_step, col_step = SIDES[side]
            if row_step == 0:
                return (out_s if out else in_s).at[0 if col_step < 0 else 1]
            if col_step == 0:
                return (out_r if out else in_r).at[0 if row_step < 0 else 1]
            return (out_c if out else in_c).at[(0 if row_step < 0 else 2) + (0 if col_step < 0 else 1)]

        copies = []
        for side, (row_step, col_step) in enumerate(SIDES):
            rows, cols = cut(HALO_ROWS, row_step), cut(HALO_COLS, col_step)
            for t in range(3):
                for which, ref in ((0, dk), (1, dv)):
                    slot(side, True)[which, t] = ref[t, rows, cols].astype(BF)
            copies.append(send(slot(side, True), slot(7 - side, False), ssem.at[side], rsem.at[side], beside(row_step, col_step)))
        for side, (row_step, col_step) in enumerate(SIDES):
            copies[side].wait_recv()
            r0, nr = OWN_ROWS[-row_step]
            c0, nc = OWN_COLS[-col_step]
            for t in range(3):
                for which, ref in ((0, dk), (1, dv)):
                    ref[t, 6 + r0 : 6 + r0 + nr, 8 + c0 : 8 + c0 + nc] += slot(7 - side, False)[which, t].astype(F32)
        for t in range(3):
            for first, ref in ((768, dk), (1536, dv)):
                gp_ref[:, :, first + 256 * t : first + 256 * t + 256] = ref[t, 6:22, 8:40].astype(BF)
        for copy in copies:
            copy.wait_send()

    vmem = pl.BlockSpec(memory_space=pltpu.VMEM)
    return pl.pallas_call(
        kernel,
        out_shape=(jax.ShapeDtypeStruct((16, 32, 768), BF), jax.ShapeDtypeStruct((16, 32, 2304), BF)),
        in_specs=[vmem] * 4,
        out_specs=(vmem, vmem),
        scratch_shapes=[
            pltpu.VMEM((3, 16, 32, 256), BF),
            pltpu.VMEM((3, 16, 32, 256), BF),
            pltpu.VMEM((3, 28, 48, 256), BF),
            pltpu.VMEM((3, 28, 48, 256), BF),
            pltpu.VMEM((3, 28, 48, 256), F32),
            pltpu.VMEM((3, 28, 48, 256), F32),
            pltpu.VMEM((4, 512, 128), F32),
            pltpu.VMEM((2, 2, 3, 16, 8, 256), BF),
            pltpu.VMEM((4, 2, 3, 6, 8, 256), BF),
            pltpu.VMEM((2, 2, 3, 6, 32, 256), BF),
            pltpu.VMEM((2, 2, 3, 16, 8, 256), BF),
            pltpu.VMEM((4, 2, 3, 6, 8, 256), BF),
            pltpu.VMEM((2, 2, 3, 6, 32, 256), BF),
            pltpu.SemaphoreType.DMA((8,)),
            pltpu.SemaphoreType.DMA((8,)),
        ],
        compiler_params=pltpu.CompilerParams(collective_id=2, has_side_effects=True, vmem_limit_bytes=60 << 20),
        name="attend",
    )(xext, grad_output, qkv_full, out_full)


def shards(features, grad_output, qkv_weight, out_weight):
    qkv_full, out_full, xext = gather(to_blocks(qkv_weight, out_weight), features)
    attended, grad_proj = attend(xext, grad_output, qkv_full, out_full)
    x_rows = features.reshape(-1, 768)
    grad_rows = grad_output.reshape(-1, 768)
    grad_proj = grad_proj.reshape(-1, 2304)
    grad_features = lax.dot_general(
        grad_proj, qkv_full, (((1,), (1,)), ((), ())), preferred_element_type=F32
    )
    grad_features = grad_features.astype(BF).reshape(16, 32, 768)
    first_term = lax.dot_general(x_rows, grad_proj, (((0,), (0,)), ((), ())), preferred_element_type=F32)
    second_term = lax.dot_general(
        attended.reshape(-1, 768), grad_rows, (((0,), (0,)), ((), ())), preferred_element_type=F32
    )
    my_grads = scatter(first_term, second_term)
    return (grad_features, my_grads[:, :2304], my_grads[:, 2304:])


def solution(mesh):
    placed = (P("lat", "lon", None), P("lat", "lon", None), P(("lat", "lon"), None), P(("lat", "lon"), None))
    return jax.shard_map(
        shards,
        mesh=mesh,
        in_specs=placed,
        out_specs=(P("lat", "lon", None), P(("lat", "lon"), None), P(("lat", "lon"), None)),
        check_vma=False,
    )
```

```python
import jax
import jax.numpy as jnp
from jax import lax
from jax.experimental import pallas as pl
from jax.experimental.pallas import tpu as pltpu
from jax.sharding import PartitionSpec as P

MESH = pl.DeviceIdType.MESH
BF = jnp.bfloat16
F32 = jnp.float32


def place():
    lat = lax.axis_index("lat")
    lon = lax.axis_index("lon")
    z, x_lo = lat // 2, lat % 2
    y, x_hi, core = lon // 4, (lon // 2) % 2, lon % 2
    return {"z": z, "y": y, "x": x_hi * 2 + x_lo}, core


def device(at, core):
    return (at["z"] * 2 + at["x"] % 2, at["y"] * 4 + (at["x"] // 2) * 2 + core)


def moved(at, axis, steps):
    out = dict(at)
    out[axis] = (at[axis] + steps + 4) % 4
    return out


def meet(peers):
    barrier = pltpu.get_barrier_semaphore()
    for peer in peers:
        pl.semaphore_signal(barrier, inc=1, device_id=peer, device_id_type=MESH)
    pl.semaphore_wait(barrier, len(peers))


def torus_peers(at, core):
    peers = [device(at, 1 - core)]
    for axis in ("z", "y", "x"):
        for steps in (1, 2, 3):
            peers.append(device(moved(at, axis, steps), core))
    return peers


def region(at, full, axis=None, coord=None):
    index = []
    for name in ("z", "y", "x"):
        if name == axis:
            index.append(coord)
        elif name in full:
            index.append(slice(None))
        else:
            index.append(at[name])
    return tuple(index)


def send(src, dst, ssem, rsem, peer):
    copy = pltpu.make_async_remote_copy(
        src_ref=src, dst_ref=dst, send_sem=ssem, recv_sem=rsem, device_id=peer, device_id_type=MESH
    )
    copy.start()
    return copy


def unpack(blocks, write):
    def body(step, carry):
        z, rest = step // 4, step % 4
        x_lo, y_pair = rest // 2, rest % 2
        for unit in range(6):
            pieces = []
            for y in range(2):
                for x_hi in range(2):
                    for core in range(2):
                        piece = blocks[core, unit, z, 2 * y_pair + y, 2 * x_hi + x_lo]
                        pieces.append(piece.astype(F32).reshape(24, 128))
            for chunk in range(4):
                rows = jnp.concatenate([p[6 * chunk : 6 * chunk + 6] for p in pieces], axis=0)
                write(step, 4 * unit + chunk, rows.astype(BF))
        return carry

    lax.fori_loop(0, 16, body, 0)


GATHER_PARTS = ((0, 4, "z", "y"), (4, 2, "y", "z"))


def gather(own, features):
    def kernel(
        own_ref, x_ref, qkv_ref, out_ref, ext_ref, blocks, sem1, sem2, sem3, psem, local_sem, hssem, hrsem
    ):
        at, core = place()
        z, y, x = at["z"], at["y"], at["x"]
        local = pltpu.make_async_copy(own_ref, blocks.at[core, :, z, y, x], local_sem.at[0])
        local.start()
        inner = pltpu.make_async_copy(x_ref, ext_ref.at[6:22, 8:40], local_sem.at[1])
        inner.start()
        meet(torus_peers(at, core) + neighbours())
        partner = device(at, 1 - core)
        sent = []
        first = []
        for k in range(3):
            first.append(
                send(
                    own_ref, blocks.at[core, :, z, y, x], sem1.at[0, k], sem1.at[1, k],
                    device(moved(at, "x", k + 1), core),
                )
            )
        halos = []
        for side, (row_step, col_step) in enumerate(SIDES):
            src = x_ref.at[cut(OWN_ROWS, row_step), cut(OWN_COLS, col_step)]
            dst = ext_ref.at[cut(HALO_ROWS, -row_step), cut(HALO_COLS, -col_step)]
            halos.append(send(src, dst, hssem.at[side], hrsem.at[side], beside(row_step, col_step)))
        local.wait()
        for copy in first:
            copy.wait_recv()
        second = {}
        for part, (unit, count, axis, _) in enumerate(GATHER_PARTS):
            where = (core, slice(unit, unit + count)) + region(at, "x")
            for k in range(3):
                second[part, k] = send(
                    blocks.at[where], blocks.at[where], sem2.at[0, part, k], sem2.at[1, part, k],
                    device(moved(at, axis, k + 1), core),
                )
        third, passed = {}, []

        def hand(part, k, where):
            passed.append(
                send(blocks.at[where], blocks.at[where], psem.at[0, part, k], psem.at[1, part, k], partner)
            )

        for part, (unit, count, axis, last) in enumerate(GATHER_PARTS):
            for k in range(3):
                second[part, k].wait_recv()
            where = (core, slice(unit, unit + count)) + region(at, ("x", axis), last, at[last])
            for k, steps in ((0, 1), (1, -1)):
                third[part, k] = send(
                    blocks.at[where], blocks.at[where], sem3.at[0, part, k], sem3.at[1, part, k],
                    device(moved(at, last, steps), core),
                )
            hand(part, 0, where)
        for part, (unit, count, axis, last) in enumerate(GATHER_PARTS):
            for k, steps in ((0, 1), (1, -1)):
                third[part, k].wait_recv()
                back = region(at, ("x", axis), last, (at[last] - steps + 4) % 4)
                half = count // 2
                where = (core, slice(unit + k * half, unit + k * half + half)) + back
                third[part, 2 + k] = send(
                    blocks.at[where], blocks.at[where], sem3.at[0, part, 2 + k], sem3.at[1, part, 2 + k],
                    device(moved(at, last, steps), core),
                )
                hand(part, 1 + k, (core, slice(unit, unit + count)) + back)
        for part, (unit, count, axis, last) in enumerate(GATHER_PARTS):
            half = count // 2
            far = region(at, ("x", axis), last, (at[last] + 2) % 4)
            for k in range(2):
                third[part, 2 + k].wait_recv()
                hand(part, 3 + k, (core, slice(unit + k * half, unit + k * half + half)) + far)
        for copy in passed:
            copy.wait_recv()

        def write(step, chunk, rows):
            first_row = pl.multiple_of(step * 48, 16)
            if chunk < 18:
                qkv_ref[pl.ds(first_row, 48), 128 * chunk : 128 * chunk + 128] = rows
            else:
                chunk -= 18
                out_ref[pl.ds(first_row, 48), 128 * chunk : 128 * chunk + 128] = rows

        unpack(blocks, write)
        for copy in halos:
            copy.wait_recv()
        for copy in halos + first + list(second.values()) + list(third.values()) + passed:
            copy.wait_send()
        inner.wait()

    vmem = pl.BlockSpec(memory_space=pltpu.VMEM)
    return pl.pallas_call(
        kernel,
        out_shape=(
            jax.ShapeDtypeStruct((768, 2304), BF),
            jax.ShapeDtypeStruct((768, 768), BF),
            jax.ShapeDtypeStruct((28, 48, 768), BF),
        ),
        in_specs=[vmem, vmem],
        out_specs=(vmem, vmem, vmem),
        scratch_shapes=[
            pltpu.VMEM((2, 6, 4, 4, 4, 3, 8, 128), BF),
            pltpu.SemaphoreType.DMA((2, 3)),
            pltpu.SemaphoreType.DMA((2, 2, 3)),
            pltpu.SemaphoreType.DMA((2, 2, 4)),
            pltpu.SemaphoreType.DMA((2, 2, 5)),
            pltpu.SemaphoreType.DMA((2,)),
            pltpu.SemaphoreType.DMA((8,)),
            pltpu.SemaphoreType.DMA((8,)),
        ],
        compiler_params=pltpu.CompilerParams(collective_id=0, has_side_effects=True),
        name="gather_weights",
    )(own, features)


def to_blocks(qkv, out):
    rows = jnp.concatenate([qkv, out], axis=1)
    rows = rows.reshape(6, 6, 4, 128).transpose(1, 2, 0, 3)
    return rows.reshape(6, 3, 8, 128)


def from_blocks(blocks):
    rows = blocks.reshape(6, 4, 6, 128).transpose(2, 0, 1, 3)
    return rows.reshape(6, 3072)


SCATTER_ORDERS = (("z", "y", "x"), ("x", "z", "y"), ("y", "x", "z"))


def scatter(first, second):
    def kernel(
        qkv_ref, out_ref, own_ref, blocks, pair_in, half_in, whole_in, mid_in, last_in, psem, ssem, msem, lsem
    ):
        at, core = place()
        meet(torus_peers(at, core))
        partner = device(at, 1 - core)

        def pack(part):
            def body(step, carry):
                z, rest = step // 4, step % 4
                x_lo, y_pair = rest // 2, rest % 2
                first_row = pl.multiple_of(step * 48, 16)
                for unit in (2 * part, 2 * part + 1):
                    chunks = []
                    for q in range(4):
                        c = 4 * unit + q
                        ref, c = (qkv_ref, c) if c < 18 else (out_ref, c - 18)
                        chunks.append(ref[pl.ds(first_row, 48), 128 * c : 128 * c + 128])
                    for e in range(8):
                        y, x_hi, to = e // 4, (e // 2) % 2, e % 2
                        rows = jnp.concatenate([c[6 * e : 6 * e + 6] for c in chunks], axis=0)
                        blocks[to, unit, z, 2 * y_pair + y, 2 * x_hi + x_lo] = rows.reshape(3, 8, 128).astype(BF)
                return carry

            lax.fori_loop(0, 16, body, 0)

        def each(count, body):
            lax.fori_loop(0, count, lambda i, c: (body(i), c)[1], 0)

        def spot(unit, where, inner):
            inner = list(inner)
            return (core, unit) + tuple(inner.pop(0) if isinstance(w, slice) else w for w in where)

        pairs, early, late, mid, last = [], {}, {}, {}, {}
        for part in range(3):
            pack(part)
            units = slice(2 * part, 2 * part + 2)
            pairs.append(
                send(blocks.at[1 - core, units], pair_in.at[units], psem.at[0, part], psem.at[1, part], partner)
            )
        for part, (a0, a1, a2) in enumerate(SCATTER_ORDERS):
            pairs[part].wait_recv()

            def add(i, part=part):
                unit, z, y = 2 * part + i // 16, (i // 4) % 4, i % 4
                total = blocks[core, unit, z, y].astype(F32) + pair_in[unit, z, y].astype(F32)
                blocks[core, unit, z, y] = total.astype(BF)

            each(32, add)
            far = region(at, (a1, a2), a0, (at[a0] + 2) % 4)
            for k, steps in ((0, 1), (1, -1)):
                early[part, k] = send(
                    blocks.at[(core, 2 * part + k) + far], half_in.at[part, k], ssem.at[0, part, k],
                    ssem.at[1, part, k], device(moved(at, a0, steps), core),
                )
        for part, (a0, a1, a2) in enumerate(SCATTER_ORDERS):
            for k, steps in ((0, 1), (1, -1)):
                early[part, k].wait_recv()
                near = region(at, (a1, a2), a0, (at[a0] + steps + 4) % 4)

                def add(i, part=part, k=k, near=near):
                    here = spot(2 * part + k, near, (i // 4, i % 4))
                    total = blocks[here].astype(F32) + half_in[part, k, i // 4, i % 4].astype(F32)
                    blocks[here] = total.astype(BF)

                each(16, add)
                late[part, k] = send(
                    blocks.at[(core, slice(2 * part, 2 * part + 2)) + near], whole_in.at[part, k],
                    ssem.at[0, part, 2 + k], ssem.at[1, part, 2 + k], device(moved(at, a0, steps), core),
                )
        for part, (a0, a1, a2) in enumerate(SCATTER_ORDERS):
            late[part, 0].wait_recv()
            late[part, 1].wait_recv()
            mine = region(at, (a1, a2), a0, at[a0])

            def add(i, part=part, mine=mine):
                j, p, q = i // 16, (i // 4) % 4, i % 4
                here = spot(2 * part + j, mine, (p, q))
                total = blocks[here].astype(F32) + whole_in[part, 0, j, p, q].astype(F32)
                blocks[here] = (total + whole_in[part, 1, j, p, q].astype(F32)).astype(BF)

            each(32, add)
            for k in range(3):
                where = region(at, (a2,), a1, (at[a1] + k + 1) % 4)
                mid[part, k] = send(
                    blocks.at[(core, slice(2 * part, 2 * part + 2)) + where], mid_in.at[part, k],
                    msem.at[0, part, k], msem.at[1, part, k], device(moved(at, a1, k + 1), core),
                )
        for part, (a0, a1, a2) in enumerate(SCATTER_ORDERS):
            for k in range(3):
                mid[part, k].wait_recv()
            mine = region(at, (a2,), a1, at[a1])
            for i in range(8):
                j, p = i // 4, i % 4
                here = spot(2 * part + j, mine, (p,))
                total = blocks[here].astype(F32)
                for k in range(3):
                    total = total + mid_in[part, k, j, p].astype(F32)
                blocks[here] = total.astype(BF)
            for k in range(3):
                where = region(at, (), a2, (at[a2] + k + 1) % 4)
                last[part, k] = send(
                    blocks.at[(core, slice(2 * part, 2 * part + 2)) + where], last_in.at[part, k],
                    lsem.at[0, part, k], lsem.at[1, part, k], device(moved(at, a2, k + 1), core),
                )
        for part in range(3):
            for k in range(3):
                last[part, k].wait_recv()
            for j in range(2):
                total = blocks[(core, 2 * part + j) + region(at, ())].astype(F32)
                for k in range(3):
                    total = total + last_in[part, k, j].astype(F32)
                own_ref[2 * part + j] = total
        for copies in (early, late, mid, last):
            for copy in copies.values():
                copy.wait_send()
        for copy in pairs:
            copy.wait_send()

    vmem = pl.BlockSpec(memory_space=pltpu.VMEM)
    tail = (3, 8, 128)
    own = pl.pallas_call(
        kernel,
        out_shape=jax.ShapeDtypeStruct((6,) + tail, F32),
        in_specs=[vmem, vmem],
        out_specs=vmem,
        scratch_shapes=[
            pltpu.VMEM((2, 6, 4, 4, 4) + tail, BF),
            pltpu.VMEM((6, 4, 4, 4) + tail, BF),
            pltpu.VMEM((3, 2, 4, 4) + tail, BF),
            pltpu.VMEM((3, 2, 2, 4, 4) + tail, BF),
            pltpu.VMEM((3, 3, 2, 4) + tail, BF),
            pltpu.VMEM((3, 3, 2) + tail, BF),
            pltpu.SemaphoreType.DMA((2, 3)),
            pltpu.SemaphoreType.DMA((2, 3, 4)),
            pltpu.SemaphoreType.DMA((2, 3, 3)),
            pltpu.SemaphoreType.DMA((2, 3, 3)),
        ],
        compiler_params=pltpu.CompilerParams(collective_id=1, has_side_effects=True, vmem_limit_bytes=60 << 20),
        name="scatter_grads",
    )(first, second)
    return from_blocks(own)


RADIUS = 6
SIDES = ((-1, -1), (-1, 0), (-1, 1), (0, -1), (0, 1), (1, -1), (1, 0), (1, 1))
OWN_ROWS = {-1: (0, 6), 0: (0, 16), 1: (10, 6)}
OWN_COLS = {-1: (0, 8), 0: (0, 32), 1: (24, 8)}
HALO_ROWS = {-1: (0, 6), 0: (6, 16), 1: (22, 6)}
HALO_COLS = {-1: (0, 8), 0: (8, 32), 1: (40, 8)}


def cut(table, step):
    first, count = table[step]
    return slice(first, first + count)


def beside(row_step, col_step):
    lat = (lax.axis_index("lat") + row_step + 8) % 8
    lon = (lax.axis_index("lon") + col_step + 16) % 16
    return (lat, lon)


def neighbours():
    return [beside(a, b) for a, b in SIDES]


def window_bias(bias, start_of):
    lat = lax.axis_index("lat")
    shape = (32, 32, 128)

    def body(i, carry):
        group, part = i // 8, i % 8
        key_row = lat * 16 + start_of(group) - 6 + part * 2 + lax.broadcasted_iota(jnp.int32, (2, 32, 128), 0)
        key_col = lax.broadcasted_iota(jnp.int32, (2, 32, 128), 1)
        lane = lax.broadcasted_iota(jnp.int32, (2, 32, 128), 2) & 63
        query_row = lat * 16 + group * 4 + (lane >> 4)
        first = jnp.clip(query_row - RADIUS, 0, 128 - 2 * RADIUS - 1)
        apart = key_col - 8 - (lane & 15)
        good = (key_row >= first) & (key_row <= first + 2 * RADIUS) & (apart >= -RADIUS) & (apart <= RADIUS)
        bias[group, pl.ds(part * 64, 64)] = jnp.where(good, 0.0, -1e30).astype(F32).reshape(64, 128)
        return carry

    lax.fori_loop(0, 32, body, 0)


def dot(a, b, left, right):
    return lax.dot_general(a, b, (((left,), (right,)), ((), ())), preferred_element_type=F32)


def spread(rows):
    head = lax.broadcasted_iota(jnp.int32, (64, 256), 1) >> 6
    return jnp.concatenate([jnp.where(head == h, rows, 0) for h in range(4)], axis=0)


def gathered(full):
    head = lax.broadcasted_iota(jnp.int32, (64, 256), 1) >> 6
    out = full[0:64]
    for h in range(1, 4):
        out = jnp.where(head == h, full[64 * h : 64 * h + 64], out)
    return out


def attend(xext, grad_output, qkv_full, out_full):
    def kernel(
        x_ref, go_ref, wqkv_ref, wout_ref, att_ref, gp_ref, q, g, k, v, dk, dv, bias, out_s, out_c, out_r, in_s, in_c,
        in_r, ssem, rsem,
    ):
        lat = lax.axis_index("lat")
        low = jnp.where(lat == 0, 4, 0)
        high = jnp.where(lat == 7, 8, 12)

        def start_of(group):
            return jnp.clip(group * 4, low, high)

        meet(neighbours())
        window_bias(bias, start_of)

        def project_own(i, carry):
            rows = x_ref[pl.ds(6 + 4 * i, 4), 8:40].reshape(128, 768)
            grads = go_ref[pl.ds(4 * i, 4)].reshape(128, 768)
            for t in range(3):
                cols = slice(256 * t, 256 * t + 256)
                head = dot(rows, wqkv_ref[:, cols], 1, 0).astype(BF).astype(F32) * 0.125
                q[t, pl.ds(4 * i, 4)] = head.astype(BF).reshape(4, 32, 256)
                head = dot(grads, wout_ref[cols, :], 1, 1).astype(BF)
                g[t, pl.ds(4 * i, 4)] = head.reshape(4, 32, 256)
            return carry

        lax.fori_loop(0, 4, project_own, 0)

        def project_all(i, carry):
            rows = x_ref[pl.ds(4 * i, 4)].reshape(192, 768)
            for t in range(3):
                for ref, first in ((k, 768), (v, 1536)):
                    cols = slice(first + 256 * t, first + 256 * t + 256)
                    ref[t, pl.ds(4 * i, 4)] = dot(rows, wqkv_ref[:, cols], 1, 0).astype(BF).reshape(4, 48, 256)
            for t in range(3):
                dk[t, pl.ds(4 * i, 4)] = jnp.zeros((4, 48, 256), F32)
                dv[t, pl.ds(4 * i, 4)] = jnp.zeros((4, 48, 256), F32)
            return carry

        lax.fori_loop(0, 7, project_all, 0)

        def tile(t, group):
            start = start_of(group)
            lanes = pl.ds(pl.multiple_of(t * 256, 256), 256)
            mask = bias[group]
            mask = jnp.concatenate([mask, mask], axis=1)
            for j in range(2):
                q_cols, k_cols = slice(16 * j, 16 * j + 16), slice(16 * j, 16 * j + 32)
                q_b = spread(q[t, pl.ds(4 * group, 4), q_cols].reshape(64, 256))
                g_b = spread(g[t, pl.ds(4 * group, 4), q_cols].reshape(64, 256))
                k4 = k[t, pl.ds(start, 16), k_cols].reshape(512, 256)
                v4 = v[t, pl.ds(start, 16), k_cols].reshape(512, 256)
                scores = dot(k4, q_b, 1, 1) + mask
                top = jnp.max(scores, axis=0, keepdims=True)
                terms = jnp.exp(scores - top)
                probs = terms * (1.0 / jnp.sum(terms, axis=0, keepdims=True))
                probs_b = probs.astype(BF)
                att = gathered(dot(probs_b, v4, 0, 0)).astype(BF)
                att_ref[pl.ds(4 * group, 4), q_cols, lanes] = att.reshape(4, 16, 256)
                dprob = dot(v4, g_b, 1, 1)
                row_term = jnp.sum(probs * dprob, axis=0, keepdims=True)
                dscore = (probs * (dprob - row_term)).astype(BF)
                dq = gathered(dot(dscore, k4, 0, 0)) * 0.125
                gp_ref[pl.ds(4 * group, 4), q_cols, lanes] = dq.astype(BF).reshape(4, 16, 256)
                dk[t, pl.ds(start, 16), k_cols] += dot(dscore, q_b, 1, 0).reshape(16, 32, 256)
                dv[t, pl.ds(start, 16), k_cols] += dot(probs_b, g_b, 1, 0).reshape(16, 32, 256)

        def slot(side, out, t):
            row_step, col_step = SIDES[side]
            if row_step == 0:
                return (out_s if out else in_s).at[0 if col_step < 0 else 1, t]
            if col_step == 0:
                return (out_r if out else in_r).at[0 if row_step < 0 else 1, t]
            return (out_c if out else in_c).at[(0 if row_step < 0 else 2) + (0 if col_step < 0 else 1), t]

        def message(side, t):
            return pltpu.make_async_remote_copy(
                src_ref=slot(side, True, t),
                dst_ref=slot(7 - side, False, t),
                send_sem=ssem.at[side, t],
                recv_sem=rsem.at[side, t],
                device_id=beside(*SIDES[side]),
                device_id_type=MESH,
            )

        def emit(sides, t):
            for side in sides:
                rows, cols = cut(HALO_ROWS, SIDES[side][0]), cut(HALO_COLS, SIDES[side][1])
                for which, ref in ((0, dk), (1, dv)):
                    slot(side, True, t)[which] = ref[t, rows, cols].astype(BF)
                message(side, t).start()

        def heads(t, carry):
            lax.fori_loop(0, 2, lambda i, c: (tile(t, i), c)[1], 0)
            emit((1, 0, 2), t)
            lax.fori_loop(2, 4, lambda i, c: (tile(t, i), c)[1], 0)
            emit((6, 5, 7, 3, 4), t)
            return carry

        lax.fori_loop(0, 3, heads, 0)

        def finish(t, carry):
            for side, (row_step, col_step) in enumerate(SIDES):
                message(side, t).wait_recv()
                r0, nr = OWN_ROWS[-row_step]
                c0, nc = OWN_COLS[-col_step]
                for which, ref in ((0, dk), (1, dv)):
                    ref[t, 6 + r0 : 6 + r0 + nr, 8 + c0 : 8 + c0 + nc] += slot(7 - side, False, t)[which].astype(F32)
            for first, ref in ((768, dk), (1536, dv)):
                lanes = pl.ds(pl.multiple_of(first + 256 * t, 256), 256)
                gp_ref[:, :, lanes] = ref[t, 6:22, 8:40].astype(BF)
            return carry

        lax.fori_loop(0, 3, finish, 0)
        for t in range(3):
            for side in range(8):
                message(side, t).wait_send()

    vmem = pl.BlockSpec(memory_space=pltpu.VMEM)
    return pl.pallas_call(
        kernel,
        out_shape=(jax.ShapeDtypeStruct((16, 32, 768), BF), jax.ShapeDtypeStruct((16, 32, 2304), BF)),
        in_specs=[vmem] * 4,
        out_specs=(vmem, vmem),
        scratch_shapes=[
            pltpu.VMEM((3, 16, 32, 256), BF),
            pltpu.VMEM((3, 16, 32, 256), BF),
            pltpu.VMEM((3, 28, 48, 256), BF),
            pltpu.VMEM((3, 28, 48, 256), BF),
            pltpu.VMEM((3, 28, 48, 256), F32),
            pltpu.VMEM((3, 28, 48, 256), F32),
            pltpu.VMEM((4, 512, 128), F32),
            pltpu.VMEM((2, 3, 2, 16, 8, 256), BF),
            pltpu.VMEM((4, 3, 2, 6, 8, 256), BF),
            pltpu.VMEM((2, 3, 2, 6, 32, 256), BF),
            pltpu.VMEM((2, 3, 2, 16, 8, 256), BF),
            pltpu.VMEM((4, 3, 2, 6, 8, 256), BF),
            pltpu.VMEM((2, 3, 2, 6, 32, 256), BF),
            pltpu.SemaphoreType.DMA((8, 3)),
            pltpu.SemaphoreType.DMA((8, 3)),
        ],
        compiler_params=pltpu.CompilerParams(collective_id=2, has_side_effects=True, vmem_limit_bytes=60 << 20),
        name="attend",
    )(xext, grad_output, qkv_full, out_full)


def shards(features, grad_output, qkv_weight, out_weight):
    qkv_full, out_full, xext = gather(to_blocks(qkv_weight, out_weight), features)
    attended, grad_proj = attend(xext, grad_output, qkv_full, out_full)
    x_rows = features.reshape(-1, 768)
    grad_rows = grad_output.reshape(-1, 768)
    grad_proj = grad_proj.reshape(-1, 2304)
    grad_features = lax.dot_general(
        grad_proj, qkv_full, (((1,), (1,)), ((), ())), preferred_element_type=F32
    )
    grad_features = grad_features.astype(BF).reshape(16, 32, 768)
    first_term = lax.dot_general(x_rows, grad_proj, (((0,), (0,)), ((), ())), preferred_element_type=F32)
    second_term = lax.dot_general(
        attended.reshape(-1, 768), grad_rows, (((0,), (0,)), ((), ())), preferred_element_type=F32
    )
    my_grads = scatter(first_term, second_term)
    return (grad_features, my_grads[:, :2304], my_grads[:, 2304:])


def solution(mesh):
    placed = (P("lat", "lon", None), P("lat", "lon", None), P(("lat", "lon"), None), P(("lat", "lon"), None))
    return jax.shard_map(
        shards,
        mesh=mesh,
        in_specs=placed,
        out_specs=(P("lat", "lon", None), P(("lat", "lon"), None), P(("lat", "lon"), None)),
        check_vma=False,
    )
```

```python
import jax
import jax.numpy as jnp
from jax import lax
from jax.experimental import pallas as pl
from jax.experimental.pallas import tpu as pltpu
from jax.sharding import PartitionSpec as P

MESH = pl.DeviceIdType.MESH
BF = jnp.bfloat16
F32 = jnp.float32


def place():
    lat = lax.axis_index("lat")
    lon = lax.axis_index("lon")
    z, x_lo = lat // 2, lat % 2
    y, x_hi, core = lon // 4, (lon // 2) % 2, lon % 2
    return {"z": z, "y": y, "x": x_hi * 2 + x_lo}, core


def device(at, core):
    return (at["z"] * 2 + at["x"] % 2, at["y"] * 4 + (at["x"] // 2) * 2 + core)


def moved(at, axis, steps):
    out = dict(at)
    out[axis] = (at[axis] + steps + 4) % 4
    return out


def meet(peers):
    barrier = pltpu.get_barrier_semaphore()
    for peer in peers:
        pl.semaphore_signal(barrier, inc=1, device_id=peer, device_id_type=MESH)
    pl.semaphore_wait(barrier, len(peers))


def torus_peers(at, core):
    peers = [device(at, 1 - core)]
    for axis in ("z", "y", "x"):
        for steps in (1, 2, 3):
            peers.append(device(moved(at, axis, steps), core))
    return peers


def region(at, full, axis=None, coord=None):
    index = []
    for name in ("z", "y", "x"):
        if name == axis:
            index.append(coord)
        elif name in full:
            index.append(slice(None))
        else:
            index.append(at[name])
    return tuple(index)


def send(src, dst, ssem, rsem, peer):
    copy = pltpu.make_async_remote_copy(
        src_ref=src, dst_ref=dst, send_sem=ssem, recv_sem=rsem, device_id=peer, device_id_type=MESH
    )
    copy.start()
    return copy


def unpack(blocks, write):
    def body(step, carry):
        z, rest = step // 4, step % 4
        x_lo, y_pair = rest // 2, rest % 2
        for unit in range(6):
            pieces = []
            for y in range(2):
                for x_hi in range(2):
                    for core in range(2):
                        piece = blocks[core, unit, z, 2 * y_pair + y, 2 * x_hi + x_lo]
                        pieces.append(piece.astype(F32).reshape(24, 128))
            for chunk in range(4):
                rows = jnp.concatenate([p[6 * chunk : 6 * chunk + 6] for p in pieces], axis=0)
                write(step, 4 * unit + chunk, rows.astype(BF))
        return carry

    lax.fori_loop(0, 16, body, 0)


GATHER_PARTS = ((0, 4, "z", "y"), (4, 2, "y", "z"))


def gather(own, features):
    def kernel(
        own_ref, x_ref, qkv_ref, out_ref, ext_ref, blocks, sem1, sem2, sem3, psem, local_sem, hssem, hrsem
    ):
        at, core = place()
        z, y, x = at["z"], at["y"], at["x"]
        local = pltpu.make_async_copy(own_ref, blocks.at[core, :, z, y, x], local_sem.at[0])
        local.start()
        inner = pltpu.make_async_copy(x_ref, ext_ref.at[6:22, 8:40], local_sem.at[1])
        inner.start()
        meet(torus_peers(at, core) + neighbours())
        partner = device(at, 1 - core)
        sent = []
        first = []
        for k in range(3):
            first.append(
                send(
                    own_ref, blocks.at[core, :, z, y, x], sem1.at[0, k], sem1.at[1, k],
                    device(moved(at, "x", k + 1), core),
                )
            )
        halos = []
        for side, (row_step, col_step) in enumerate(SIDES):
            src = x_ref.at[cut(OWN_ROWS, row_step), cut(OWN_COLS, col_step)]
            dst = ext_ref.at[cut(HALO_ROWS, -row_step), cut(HALO_COLS, -col_step)]
            halos.append(send(src, dst, hssem.at[side], hrsem.at[side], beside(row_step, col_step)))
        local.wait()
        for copy in first:
            copy.wait_recv()
        second = {}
        for part, (unit, count, axis, _) in enumerate(GATHER_PARTS):
            where = (core, slice(unit, unit + count)) + region(at, "x")
            for k in range(3):
                second[part, k] = send(
                    blocks.at[where], blocks.at[where], sem2.at[0, part, k], sem2.at[1, part, k],
                    device(moved(at, axis, k + 1), core),
                )
        third, passed = {}, []

        def hand(part, k, where):
            passed.append(
                send(blocks.at[where], blocks.at[where], psem.at[0, part, k], psem.at[1, part, k], partner)
            )

        for part, (unit, count, axis, last) in enumerate(GATHER_PARTS):
            for k in range(3):
                second[part, k].wait_recv()
            where = (core, slice(unit, unit + count)) + region(at, ("x", axis), last, at[last])
            for k, steps in ((0, 1), (1, -1)):
                third[part, k] = send(
                    blocks.at[where], blocks.at[where], sem3.at[0, part, k], sem3.at[1, part, k],
                    device(moved(at, last, steps), core),
                )
            hand(part, 0, where)
        for part, (unit, count, axis, last) in enumerate(GATHER_PARTS):
            for k, steps in ((0, 1), (1, -1)):
                third[part, k].wait_recv()
                back = region(at, ("x", axis), last, (at[last] - steps + 4) % 4)
                half = count // 2
                where = (core, slice(unit + k * half, unit + k * half + half)) + back
                third[part, 2 + k] = send(
                    blocks.at[where], blocks.at[where], sem3.at[0, part, 2 + k], sem3.at[1, part, 2 + k],
                    device(moved(at, last, steps), core),
                )
                hand(part, 1 + k, (core, slice(unit, unit + count)) + back)
        for part, (unit, count, axis, last) in enumerate(GATHER_PARTS):
            half = count // 2
            far = region(at, ("x", axis), last, (at[last] + 2) % 4)
            for k in range(2):
                third[part, 2 + k].wait_recv()
                hand(part, 3 + k, (core, slice(unit + k * half, unit + k * half + half)) + far)
        for copy in passed:
            copy.wait_recv()

        def write(step, chunk, rows):
            first_row = pl.multiple_of(step * 48, 16)
            if chunk < 18:
                qkv_ref[pl.ds(first_row, 48), 128 * chunk : 128 * chunk + 128] = rows
            else:
                chunk -= 18
                out_ref[pl.ds(first_row, 48), 128 * chunk : 128 * chunk + 128] = rows

        unpack(blocks, write)
        for copy in halos:
            copy.wait_recv()
        for copy in halos + first + list(second.values()) + list(third.values()) + passed:
            copy.wait_send()
        inner.wait()

    vmem = pl.BlockSpec(memory_space=pltpu.VMEM)
    return pl.pallas_call(
        kernel,
        out_shape=(
            jax.ShapeDtypeStruct((768, 2304), BF),
            jax.ShapeDtypeStruct((768, 768), BF),
            jax.ShapeDtypeStruct((28, 48, 768), BF),
        ),
        in_specs=[vmem, vmem],
        out_specs=(vmem, vmem, vmem),
        scratch_shapes=[
            pltpu.VMEM((2, 6, 4, 4, 4, 3, 8, 128), BF),
            pltpu.SemaphoreType.DMA((2, 3)),
            pltpu.SemaphoreType.DMA((2, 2, 3)),
            pltpu.SemaphoreType.DMA((2, 2, 4)),
            pltpu.SemaphoreType.DMA((2, 2, 5)),
            pltpu.SemaphoreType.DMA((2,)),
            pltpu.SemaphoreType.DMA((8,)),
            pltpu.SemaphoreType.DMA((8,)),
        ],
        compiler_params=pltpu.CompilerParams(collective_id=0, has_side_effects=True),
        name="gather_weights",
    )(own, features)


def to_blocks(qkv, out):
    rows = jnp.concatenate([qkv, out], axis=1)
    rows = rows.reshape(6, 6, 4, 128).transpose(1, 2, 0, 3)
    return rows.reshape(6, 3, 8, 128)


RADIUS = 6
SIDES = ((-1, -1), (-1, 0), (-1, 1), (0, -1), (0, 1), (1, -1), (1, 0), (1, 1))
OWN_ROWS = {-1: (0, 6), 0: (0, 16), 1: (10, 6)}
OWN_COLS = {-1: (0, 8), 0: (0, 32), 1: (24, 8)}
HALO_ROWS = {-1: (0, 6), 0: (6, 16), 1: (22, 6)}
HALO_COLS = {-1: (0, 8), 0: (8, 32), 1: (40, 8)}


def cut(table, step):
    first, count = table[step]
    return slice(first, first + count)


def beside(row_step, col_step):
    lat = (lax.axis_index("lat") + row_step + 8) % 8
    lon = (lax.axis_index("lon") + col_step + 16) % 16
    return (lat, lon)


def neighbours():
    return [beside(a, b) for a, b in SIDES]


def window_bias(bias, start_of):
    lat = lax.axis_index("lat")
    shape = (32, 32, 128)

    def body(i, carry):
        group, part = i // 8, i % 8
        key_row = lat * 16 + start_of(group) - 6 + part * 2 + lax.broadcasted_iota(jnp.int32, (2, 32, 128), 0)
        key_col = lax.broadcasted_iota(jnp.int32, (2, 32, 128), 1)
        lane = lax.broadcasted_iota(jnp.int32, (2, 32, 128), 2) & 63
        query_row = lat * 16 + group * 4 + (lane >> 4)
        first = jnp.clip(query_row - RADIUS, 0, 128 - 2 * RADIUS - 1)
        apart = key_col - 8 - (lane & 15)
        good = (key_row >= first) & (key_row <= first + 2 * RADIUS) & (apart >= -RADIUS) & (apart <= RADIUS)
        bias[group, pl.ds(part * 64, 64)] = jnp.where(good, 0.0, -1e30).astype(F32).reshape(64, 128)
        return carry

    lax.fori_loop(0, 32, body, 0)


def dot(a, b, left, right):
    return lax.dot_general(a, b, (((left,), (right,)), ((), ())), preferred_element_type=F32)


def spread(rows):
    head = lax.broadcasted_iota(jnp.int32, (64, 256), 1) >> 6
    return jnp.concatenate([jnp.where(head == h, rows, 0) for h in range(4)], axis=0)


def gathered(full):
    head = lax.broadcasted_iota(jnp.int32, (64, 256), 1) >> 6
    out = full[0:64]
    for h in range(1, 4):
        out = jnp.where(head == h, full[64 * h : 64 * h + 64], out)
    return out


def chunk_column(i):
    return 768 * (i % 3) + 256 * (i // 3) if i < 9 else 256 * (i - 9)


SCATTER_ORDERS = (("x", "y", "z"), ("y", "z", "x"), ("z", "y", "x"))


def attend(xext, grad_output, qkv_full, out_full):
    def kernel(
        x_ref, go_ref, wqkv_ref, wout_ref, gx_ref, gqkv_ref, gout_ref,
        q, g, k, v, dk, dv, bias, att, dq, dkv, xt, xo, dw, dx, out_s, out_c, out_r, in_s, in_c, in_r,
        blocks, pair_in, half_in, whole_in, mid_in, last_in, hsem, psem, ssem, msem, lsem,
    ):
        at, core = place()
        partner = device(at, 1 - core)
        lat = lax.axis_index("lat")
        low = jnp.where(lat == 0, 4, 0)
        high = jnp.where(lat == 7, 8, 12)

        def start_of(group):
            return jnp.clip(group * 4, low, high)

        def each(count, body):
            lax.fori_loop(0, count, lambda i, c: (body(i), c)[1], 0)

        meet(torus_peers(at, core) + neighbours())
        window_bias(bias, start_of)

        def project_own(t):
            lanes = pl.ds(pl.multiple_of(256 * t, 256), 256)
            rows = x_ref[6:22, 8:40].reshape(512, 768)
            head = dot(rows, wqkv_ref[:, lanes], 1, 0).astype(BF).astype(F32) * 0.125
            q[t] = head.astype(BF).reshape(16, 32, 256)
            grads = go_ref[...].reshape(512, 768)
            g[t] = dot(grads, wout_ref[lanes, :], 1, 1).astype(BF).reshape(16, 32, 256)

        each(3, project_own)

        def project_all(i):
            t, half = i // 2, pl.ds(14 * (i % 2), 14)
            rows = x_ref[half].reshape(672, 768)
            for ref, first in ((k, 768), (v, 1536)):
                lanes = pl.ds(pl.multiple_of(first + 256 * t, 256), 256)
                ref[t, half] = dot(rows, wqkv_ref[:, lanes], 1, 0).astype(BF).reshape(14, 48, 256)

        each(6, project_all)
        for i in range(6):
            lanes = slice(128 * i, 128 * i + 128)
            xt[lanes] = x_ref[:, :, lanes].reshape(1344, 128).T
            xo[lanes] = x_ref[6:22, 8:40, lanes].reshape(512, 128).T

        def tile(t, group):
            start = start_of(group)
            lanes = slice(256 * t, 256 * t + 256)
            mask = bias[group]
            mask = jnp.concatenate([mask, mask], axis=1)
            for j in range(2):
                q_cols, k_cols = slice(16 * j, 16 * j + 16), slice(16 * j, 16 * j + 32)
                q_b = spread(q[t, pl.ds(4 * group, 4), q_cols].reshape(64, 256))
                g_b = spread(g[t, pl.ds(4 * group, 4), q_cols].reshape(64, 256))
                k4 = k[t, pl.ds(start, 16), k_cols].reshape(512, 256)
                v4 = v[t, pl.ds(start, 16), k_cols].reshape(512, 256)
                scores = dot(k4, q_b, 1, 1) + mask
                top = jnp.max(scores, axis=0, keepdims=True)
                terms = jnp.exp(scores - top)
                probs = terms * (1.0 / jnp.sum(terms, axis=0, keepdims=True))
                probs_b = probs.astype(BF)
                out = gathered(dot(probs_b, v4, 0, 0)).astype(BF)
                att[pl.ds(4 * group, 4), q_cols, lanes] = out.reshape(4, 16, 256)
                dprob = dot(v4, g_b, 1, 1)
                row_term = jnp.sum(probs * dprob, axis=0, keepdims=True)
                dscore = (probs * (dprob - row_term)).astype(BF)
                out = gathered(dot(dscore, k4, 0, 0)) * 0.125
                dq[pl.ds(4 * group, 4), q_cols, lanes] = out.astype(BF).reshape(4, 16, 256)
                dk[pl.ds(start, 16), k_cols] += dot(dscore, q_b, 1, 0).reshape(16, 32, 256)
                dv[pl.ds(start, 16), k_cols] += dot(probs_b, g_b, 1, 0).reshape(16, 32, 256)

        pairs, early, late, mid, last = {}, {}, {}, {}, {}

        def begin(part):
            for i in range(4 * part, 4 * part + 4):
                to = slice(256 * (i % 4), 256 * (i % 4) + 256)
                col = chunk_column(i)

                if i >= 9:
                    left = att[...].reshape(512, 768)
                    dw[:, to] = dot(left, go_ref[:, :, col : col + 256].reshape(512, 256), 0, 0)
                elif i % 3 == 0:
                    dw[:, to] = dot(xo[...], dq[:, :, col : col + 256].reshape(512, 256), 1, 0)
                else:
                    dw[:, to] = dot(xt[...], dkv[:, :, col - 768 : col - 512].reshape(1344, 256), 1, 0)

            def pack(step):
                z, rest = step // 4, step % 4
                x_lo, y_pair = rest // 2, rest % 2
                first_row = pl.multiple_of(step * 48, 16)
                for unit in range(2):
                    chunks = []
                    for n in range(4):
                        first = 512 * unit + 128 * n
                        chunks.append(dw[pl.ds(first_row, 48), first : first + 128])
                    for e in range(8):
                        y, x_hi, to = e // 4, (e // 2) % 2, e % 2
                        rows = jnp.concatenate([c[6 * e : 6 * e + 6] for c in chunks], axis=0)
                        rows = rows.reshape(3, 8, 128).astype(BF)
                        blocks[to, 2 * part + unit, z, 2 * y_pair + y, 2 * x_hi + x_lo] = rows

            each(16, pack)
            units = slice(2 * part, 2 * part + 2)
            pairs[part] = send(
                blocks.at[1 - core, units], pair_in.at[units], psem.at[0, part], psem.at[1, part], partner
            )

        def step_pair(part):
            a0, a1, a2 = SCATTER_ORDERS[part]
            pairs[part].wait_recv()

            def add(i):
                unit, z = 2 * part + i // 4, i % 4
                total = blocks[core, unit, z].astype(F32) + pair_in[unit, z].astype(F32)
                blocks[core, unit, z] = total.astype(BF)

            each(8, add)
            far = region(at, (a1, a2), a0, (at[a0] + 2) % 4)
            for n, steps in ((0, 1), (1, -1)):
                early[part, n] = send(
                    blocks.at[(core, 2 * part + n) + far], half_in.at[part, n], ssem.at[0, part, n],
                    ssem.at[1, part, n], device(moved(at, a0, steps), core),
                )

        def step_early(part):
            a0, a1, a2 = SCATTER_ORDERS[part]
            for n, steps in ((0, 1), (1, -1)):
                early[part, n].wait_recv()
                near = region(at, (a1, a2), a0, (at[a0] + steps + 4) % 4)

                here = (core, 2 * part + n) + near
                blocks[here] = (blocks[here].astype(F32) + half_in[part, n].astype(F32)).astype(BF)
                late[part, n] = send(
                    blocks.at[(core, slice(2 * part, 2 * part + 2)) + near], whole_in.at[part, n],
                    ssem.at[0, part, 2 + n], ssem.at[1, part, 2 + n], device(moved(at, a0, steps), core),
                )

        def step_late(part):
            a0, a1, a2 = SCATTER_ORDERS[part]
            late[part, 0].wait_recv()
            late[part, 1].wait_recv()
            mine = region(at, (a1, a2), a0, at[a0])

            for j in range(2):
                here = (core, 2 * part + j) + mine
                total = blocks[here].astype(F32) + whole_in[part, 0, j].astype(F32)
                blocks[here] = (total + whole_in[part, 1, j].astype(F32)).astype(BF)
            for n in range(3):
                where = region(at, (a2,), a1, (at[a1] + n + 1) % 4)
                mid[part, n] = send(
                    blocks.at[(core, slice(2 * part, 2 * part + 2)) + where], mid_in.at[part, n],
                    msem.at[0, part, n], msem.at[1, part, n], device(moved(at, a1, n + 1), core),
                )

        def step_mid(part):
            a0, a1, a2 = SCATTER_ORDERS[part]
            for n in range(3):
                mid[part, n].wait_recv()
            mine = region(at, (a2,), a1, at[a1])
            for j in range(2):
                here = (core, 2 * part + j) + mine
                total = blocks[here].astype(F32)
                for n in range(3):
                    total = total + mid_in[part, n, j].astype(F32)
                blocks[here] = total.astype(BF)
            for n in range(3):
                where = region(at, (), a2, (at[a2] + n + 1) % 4)
                last[part, n] = send(
                    blocks.at[(core, slice(2 * part, 2 * part + 2)) + where], last_in.at[part, n],
                    lsem.at[0, part, n], lsem.at[1, part, n], device(moved(at, a2, n + 1), core),
                )

        def step_last(part):
            for n in range(3):
                last[part, n].wait_recv()
            for j in range(2):
                total = blocks[(core, 2 * part + j) + region(at, ())].astype(F32)
                for n in range(3):
                    total = total + last_in[part, n, j].astype(F32)
                total = total.reshape(24, 128)
                for n in range(4):
                    i = 4 * part + 2 * j + n // 2
                    col = chunk_column(i) + 128 * (n % 2)
                    ref = gout_ref if i >= 9 else gqkv_ref
                    ref[:, col : col + 128] = total[6 * n : 6 * n + 6]

        for t in range(3):

            def clear(i):
                dk[i] = jnp.zeros((48, 256), F32)
                dv[i] = jnp.zeros((48, 256), F32)

            each(28, clear)
            each(4, lambda group, t=t: tile(t, group))

            def store(i, t=t):
                dkv[i, :, 256 * t : 256 * t + 256] = dk[i].astype(BF)
                dkv[i, :, 768 + 256 * t : 1024 + 256 * t] = dv[i].astype(BF)

            each(28, store)
            if t == 1:
                begin(0)

        def back_edge(n):
            lanes = pl.ds(pl.multiple_of(256 * n, 256), 256)
            rows = jnp.concatenate([dkv[0:6].reshape(288, 1536), dkv[22:28].reshape(288, 1536)], axis=0)
            out = dot(rows, wqkv_ref[lanes, 768:2304], 1, 1)
            dx[0:6, :, lanes] = out[0:288].reshape(6, 48, 256)
            dx[22:28, :, lanes] = out[288:576].reshape(6, 48, 256)

        def back_inner(n):
            lanes = pl.ds(pl.multiple_of(256 * n, 256), 256)
            rows = dkv[6:22].reshape(768, 1536)
            dx[6:22, :, lanes] = dot(rows, wqkv_ref[lanes, 768:2304], 1, 1).reshape(16, 48, 256)

        def back_own(n):
            lanes = pl.ds(pl.multiple_of(256 * n, 256), 256)
            rows = dq[...].reshape(512, 768)
            dx[6:22, 8:40, lanes] += dot(rows, wqkv_ref[lanes, 0:768], 1, 1).reshape(16, 32, 256)

        def slot(side, out):
            row_step, col_step = SIDES[side]
            if row_step == 0:
                return (out_s if out else in_s).at[0 if col_step < 0 else 1]
            if col_step == 0:
                return (out_r if out else in_r).at[0 if row_step < 0 else 1]
            return (out_c if out else in_c).at[(0 if row_step < 0 else 2) + (0 if col_step < 0 else 1)]

        halos = {}

        def emit(side):
            rows, cols = cut(HALO_ROWS, SIDES[side][0]), cut(HALO_COLS, SIDES[side][1])
            slot(side, True)[...] = dx[rows, cols].astype(BF)
            halos[side] = send(
                slot(side, True), slot(7 - side, False), hsem.at[0, side], hsem.at[1, side], beside(*SIDES[side])
            )

        step_pair(0)
        each(3, back_edge)
        for side in (1, 6, 0, 2, 5, 7):
            emit(side)
        begin(1)
        step_early(0)
        begin(2)
        step_pair(1)
        each(3, back_inner)
        for side in (3, 4):
            emit(side)
        step_pair(2)
        step_late(0)
        step_early(1)
        step_early(2)
        step_mid(0)

        each(3, back_own)
        step_late(1)
        step_late(2)
        step_last(0)
        step_mid(1)
        step_mid(2)
        for side, (row_step, col_step) in enumerate(SIDES):
            halos[side].wait_recv()
            r0, nr = OWN_ROWS[-row_step]
            c0, nc = OWN_COLS[-col_step]
            dx[6 + r0 : 6 + r0 + nr, 8 + c0 : 8 + c0 + nc] += slot(7 - side, False)[...].astype(F32)

        def finish(i):
            gx_ref[pl.ds(4 * i, 4)] = dx[pl.ds(6 + 4 * i, 4), 8:40].astype(BF)

        each(4, finish)
        step_last(1)
        step_last(2)
        for copies in (pairs, early, late, mid, last, halos):
            for copy in copies.values():
                copy.wait_send()

    vmem = pl.BlockSpec(memory_space=pltpu.VMEM)
    tail = (3, 8, 128)
    return pl.pallas_call(
        kernel,
        out_shape=(
            jax.ShapeDtypeStruct((16, 32, 768), BF),
            jax.ShapeDtypeStruct((6, 2304), F32),
            jax.ShapeDtypeStruct((6, 768), F32),
        ),
        in_specs=[vmem] * 4,
        out_specs=(vmem, vmem, vmem),
        scratch_shapes=[
            pltpu.VMEM((3, 16, 32, 256), BF),
            pltpu.VMEM((3, 16, 32, 256), BF),
            pltpu.VMEM((3, 28, 48, 256), BF),
            pltpu.VMEM((3, 28, 48, 256), BF),
            pltpu.VMEM((28, 48, 256), F32),
            pltpu.VMEM((28, 48, 256), F32),
            pltpu.VMEM((4, 512, 128), F32),
            pltpu.VMEM((16, 32, 768), BF),
            pltpu.VMEM((16, 32, 768), BF),
            pltpu.VMEM((28, 48, 1536), BF),
            pltpu.VMEM((768, 1344), BF),
            pltpu.VMEM((768, 512), BF),
            pltpu.VMEM((768, 1024), F32),
            pltpu.VMEM((28, 48, 768), F32),
            pltpu.VMEM((2, 16, 8, 768), BF),
            pltpu.VMEM((4, 6, 8, 768), BF),
            pltpu.VMEM((2, 6, 32, 768), BF),
            pltpu.VMEM((2, 16, 8, 768), BF),
            pltpu.VMEM((4, 6, 8, 768), BF),
            pltpu.VMEM((2, 6, 32, 768), BF),
            pltpu.VMEM((2, 6, 4, 4, 4) + tail, BF),
            pltpu.VMEM((6, 4, 4, 4) + tail, BF),
            pltpu.VMEM((3, 2, 4, 4) + tail, BF),
            pltpu.VMEM((3, 2, 2, 4, 4) + tail, BF),
            pltpu.VMEM((3, 3, 2, 4) + tail, BF),
            pltpu.VMEM((3, 3, 2) + tail, BF),
            pltpu.SemaphoreType.DMA((2, 8)),
            pltpu.SemaphoreType.DMA((2, 3)),
            pltpu.SemaphoreType.DMA((2, 3, 4)),
            pltpu.SemaphoreType.DMA((2, 3, 3)),
            pltpu.SemaphoreType.DMA((2, 3, 3)),
        ],
        compiler_params=pltpu.CompilerParams(collective_id=1, has_side_effects=True, vmem_limit_bytes=62 << 20),
        name="attend",
    )(xext, grad_output, qkv_full, out_full)


def shards(features, grad_output, qkv_weight, out_weight):
    qkv_full, out_full, xext = gather(to_blocks(qkv_weight, out_weight), features)
    return tuple(attend(xext, grad_output, qkv_full, out_full))


def solution(mesh):
    placed = (P("lat", "lon", None), P("lat", "lon", None), P(("lat", "lon"), None), P(("lat", "lon"), None))
    return jax.shard_map(
        shards,
        mesh=mesh,
        in_specs=placed,
        out_specs=(P("lat", "lon", None), P(("lat", "lon"), None), P(("lat", "lon"), None)),
        check_vma=False,
    )
```
